32 devices in a mesh: group: 2 (over y), expert: 4 (over z), tensor: 4 (over x, core).
Axes of the slice: x: 2, y: 2, z: 4, core: 2. Of those that a mesh axis runs over, the one named last changes fastest.
Arguments:
- q_absorbed: bfloat16 [1024, 36864], P(('group', 'expert'), 'tensor'), parts along dimension 0, may hold values from -14 to 14
- kv_latent: bfloat16 [1024, 576], P(('group', 'expert')), parts along dimension 0, may hold values from -4 to 4
- w_values: bfloat16 [64, 512, 128], P('tensor'), may hold values from -1 to 1
- w_out: bfloat16 [8192, 7168], P('tensor', 'expert'), may hold values from -0.0625 to 0.0625
- layer_input: bfloat16 [1024, 7168], P(('group', 'expert')), parts along dimension 0, may hold values from -40 to 40
- norm_gain: float32 [7168], replicated, may hold values from 0.1 to 1.9
- predicted: int32 [1024, 8], P(('group', 'expert')), parts along dimension 0, may hold values from 0 to 15, as said below
- actual: int32 [1024, 8], P(('group', 'expert')), parts along dimension 0, may hold values from 0 to 15, as said below
- gates: float32 [1024, 8], P(('group', 'expert')), parts along dimension 0, may hold values from 0.1 to 1
- w_gate: bfloat16 [16, 7168, 1024], P('expert', 'tensor'), may hold values from -0.0625 to 0.0625
- w_up: bfloat16 [16, 7168, 1024], P('expert', 'tensor'), may hold values from -0.0625 to 0.0625
- w_down: bfloat16 [16, 1024, 7168], P('expert', None, 'tensor'), may hold values from -0.1875 to 0.1875
Outputs:
- attended: bfloat16 [1024, 7168], P(('group', 'expert'), 'tensor'), parts along dimension 0
- mixture: bfloat16 [1024, 7168], P(('group', 'expert'), 'tensor'), parts along dimension 0
- missed: float32 [1024], P(('group', 'expert')), parts along dimension 0
The draws below stay inside these ranges and needn't reach their ends.
There are 2 independent parts, one for each index of `group`. The reference program is written for one: setup_inputs(seed, part) draws one part's arguments, and reference() takes and returns one part's arrays. A program takes and returns all parts, laid end to end along the dimension named above; an argument that names none is the same for every part. Nothing has to cross between parts.
Inputs may be any that keep to these rules, and one draw needn't show every extreme that they name: `predicted`: each row names 8 different experts. In each aligned block of 128 rows (the rows of one index of expert) at most 80 rows name the same expert, and in every draw some expert is named by exactly 80 rows of every block. `actual`: each row names 8 different experts. In each aligned block of 128 rows (the rows of one index of expert) at most 12 rows name a given expert that the same row of predicted does not name, and in every draw some expert reaches 12 such rows in every block.
All inputs are finite; a program needn't handle non-finite values.
Results may differ from the reference program's by a relative error of at most 0.023.
Values may be sent and summed in bfloat16 or wider, within the bound.
No kernel may reach another device: no remote copies, remote signals or barrier semaphores. Data moves between devices by JAX's collectives and lax.ppermute only.
A program may use at most 128 MiB of HBM per device.

```python
import math
import jax
import jax.numpy as jnp
from jax import lax

D = 7168
LAT = 512
ROPE = 64
VDIM = 128
TOP = 8
HEADS = 64
FF = 1024
ACTIVE_EXPERTS = 16
T_DEV = 128
QK = 576
SEQUENCE_TOKENS = 512
CAP = 80
CAP_C = 12
N_EXPERT = 4
N_TENSOR = 4


def draw_kv_latent(key, part):
    base = jnp.clip(jax.random.normal(jax.random.fold_in(key, 32), (SEQUENCE_TOKENS, QK), jnp.float32), -4.0, 4.0)
    return base.astype(jnp.bfloat16)


def draw_q_absorbed(key, part):
    base = jnp.clip(1.15 * jax.random.normal(jax.random.fold_in(key, 33), (SEQUENCE_TOKENS, HEADS, QK), jnp.float32), -4.6, 4.6)
    return base.reshape(SEQUENCE_TOKENS, HEADS * QK).astype(jnp.bfloat16)


def draw_layer_input(key, part):
    row_scale = jnp.exp(jax.random.uniform(jax.random.fold_in(key, 51), (SEQUENCE_TOKENS, 1), jnp.float32, -1.15, 1.15))
    col_scale = jnp.exp(jax.random.uniform(jax.random.fold_in(key, 52), (1, D), jnp.float32, -1.15, 1.15))
    base = jnp.clip(jax.random.normal(jax.random.fold_in(key, 53), (SEQUENCE_TOKENS, D), jnp.float32), -4.0, 4.0)
    return (base * row_scale * col_scale).astype(jnp.bfloat16)


def route_plan(key):
    blocks = SEQUENCE_TOKENS // T_DEV
    spread = 3 * T_DEV // 4
    order = jax.random.permutation(jax.random.fold_in(key, 40), ACTIVE_EXPERTS)
    flag_markers = jax.random.randint(jax.random.fold_in(key, 41), (2,), 0, ACTIVE_EXPERTS)
    block_keys = jax.random.split(jax.random.fold_in(key, 42), blocks)
    rank_positions = jax.vmap(lambda block_key: jax.random.permutation(block_key, T_DEV))(block_keys).reshape(SEQUENCE_TOKENS)
    block_displacement = jnp.repeat(jax.random.randint(jax.random.fold_in(key, 43), (blocks,), 0, 2), T_DEV)
    sudden_batch = flag_markers[0] + block_displacement + jax.random.randint(jax.random.fold_in(key, 44), (SEQUENCE_TOKENS,), 0, 4)
    spread_flag = rank_positions < spread
    start_displacement = jnp.where(spread_flag, rank_positions % ACTIVE_EXPERTS, sudden_batch) % ACTIVE_EXPERTS
    near = (start_displacement == flag_markers[1] % ACTIVE_EXPERTS) | (start_displacement == (flag_markers[1] + ACTIVE_EXPERTS - 1) % ACTIVE_EXPERTS)
    random_move = jax.random.randint(jax.random.fold_in(key, 45), (SEQUENCE_TOKENS,), 0, 3)
    moved = jnp.where(spread_flag, jnp.where(near, 2, random_move), 0)
    steps = jnp.arange(TOP)
    guess = order[(start_displacement[:, None] + steps[None, :]) % ACTIVE_EXPERTS]
    truth = order[(start_displacement[:, None] + moved[:, None] + steps[None, :]) % ACTIVE_EXPERTS]
    return (guess.astype(jnp.int32), truth.astype(jnp.int32))


def draw_predicted(key, part):
    return route_plan(key)[0]


def draw_actual(key, part):
    return route_plan(key)[1]


def block_scale(key, shape, shards, least, top_value):
    gain, own = 1.0, jax.random.fold_in(key, 6)
    for position, shards_of in shards:
        steps = jnp.exp(jax.random.uniform(jax.random.fold_in(own, position), (shards_of,), jnp.float32, least / len(shards), top_value / len(shards)))
        gain = gain * jnp.repeat(steps, shape[position] // shards_of).reshape([-1 if axis == position else 1 for axis in range(len(shape))])
    return gain


def normal_values(rng, shape, scale, reach, cuts=(), kind=jnp.bfloat16):
    drawn = jax.random.normal(rng, shape, jnp.float32) * scale
    if len(cuts) > 0:
        drawn = block_scale(rng, shape, cuts, -0.22, 0.18) * drawn
    return jnp.clip(drawn, min=-reach, max=reach).astype(kind)


def setup_inputs(seed: int = 0, part: int = 0) -> dict:
    key_of = jax.random.split(jax.random.key(seed), 13)
    own_keys = jax.random.split(jax.random.fold_in(key_of[12], part), 13)
    return {
        "q_absorbed": draw_q_absorbed(jax.random.fold_in(jax.random.fold_in(key_of[12], part), 71), part),
        "kv_latent": draw_kv_latent(jax.random.fold_in(jax.random.fold_in(key_of[12], part), 71), part),
        "w_values": normal_values(key_of[2], (HEADS, LAT, VDIM), (LAT // 16) ** -0.5, 1.0, ((0, 4),)),
        "w_out": normal_values(key_of[3], (HEADS * VDIM, D), (HEADS * VDIM) ** -0.5, 0.0625, ((0, 4), (1, 4))),
        "layer_input": draw_layer_input(jax.random.fold_in(jax.random.fold_in(key_of[12], part), 71), part),
        "norm_gain": jnp.clip(1.0 + 0.18 * jax.random.normal(key_of[5], (D,), jnp.float32), 0.1, 1.9),
        "predicted": draw_predicted(jax.random.fold_in(jax.random.fold_in(key_of[12], part), 71), part),
        "actual": draw_actual(jax.random.fold_in(jax.random.fold_in(key_of[12], part), 71), part),
        "gates": jnp.clip(jnp.exp(math.log(1.0) - 2.3025851 * jax.random.uniform(own_keys[8], (SEQUENCE_TOKENS, TOP), jnp.float32) ** block_scale(own_keys[8], (SEQUENCE_TOKENS, TOP), ((0, 4),), -0.2, 0.2)), 0.1, 1.0),
        "w_gate": normal_values(key_of[9], (ACTIVE_EXPERTS, D, FF), D ** -0.5, 0.0625, ((0, 4), (1, 4))),
        "w_up": normal_values(key_of[10], (ACTIVE_EXPERTS, D, FF), D ** -0.5, 0.0625, ((0, 4), (1, 4))),
        "w_down": normal_values(key_of[11], (ACTIVE_EXPERTS, FF, D), FF ** -0.5, 0.1875, ((0, 4), (2, 4))),
    }


EPS = 1e-06

def head_attention(query, weight, kv_latent, visible, scale):
    scores = jnp.dot(query, kv_latent.T, preferred_element_type=jnp.float32) * scale
    masked = jnp.where(visible, scores, -jnp.inf)
    largest = lax.optimization_barrier(jnp.max(masked, axis=1, keepdims=True))
    expo = jnp.exp(masked - largest)
    denominator = lax.optimization_barrier(jnp.sum(expo, axis=1, keepdims=True))
    weights = expo.astype(jnp.bfloat16)
    latent = jnp.dot(weights, kv_latent[:, :LAT], preferred_element_type=jnp.float32) / denominator
    latent = latent.astype(jnp.bfloat16)
    return jnp.dot(latent, weight, preferred_element_type=jnp.float32).astype(jnp.bfloat16)

def range_sum(pieces, weight):
    blocks = weight.reshape(N_TENSOR, D // N_TENSOR, FF).astype(jnp.float32)
    terms = jnp.einsum('ntd,tdf->tnf', pieces, blocks)
    rounded = lax.optimization_barrier(terms.astype(jnp.bfloat16))
    return lax.optimization_barrier(jnp.sum(rounded.astype(jnp.float32), axis=0))

def expert_rows(picked_rows, weight_gate, weight_up, weight_down):
    count = picked_rows.shape[0]
    pieces = picked_rows.reshape(count, N_TENSOR, D // N_TENSOR).astype(jnp.float32)
    gate_pre = range_sum(pieces, weight_gate)
    up_pre = range_sum(pieces, weight_up)
    act = (jax.nn.silu(gate_pre) * up_pre).astype(jnp.bfloat16)
    return jnp.dot(act, weight_down, preferred_element_type=jnp.float32).astype(jnp.bfloat16)

def reference(q_absorbed, kv_latent, w_values, w_out, layer_input, norm_gain, predicted, actual, gates, w_gate, w_up, w_down):
    scale = (VDIM + ROPE) ** (-0.5)
    positions = jnp.arange(SEQUENCE_TOKENS, dtype=jnp.int32)
    visible = positions[:, None] >= positions[None, :]
    queries = jnp.transpose(q_absorbed.reshape(SEQUENCE_TOKENS, HEADS, QK), (1, 0, 2))

    def one_head(pair):
        return head_attention(pair[0], pair[1], kv_latent, visible, scale)
    heads_out = lax.map(one_head, (queries, w_values))
    heads_flat = jnp.transpose(heads_out, (1, 0, 2)).reshape(SEQUENCE_TOKENS, HEADS * VDIM)
    attended = jnp.dot(heads_flat, w_out, preferred_element_type=jnp.float32).astype(jnp.bfloat16)
    features = layer_input.astype(jnp.float32)
    inverse = lax.rsqrt(lax.optimization_barrier(jnp.mean(features * features, axis=1, keepdims=True)) + EPS)
    normed = (features * inverse * norm_gain).astype(jnp.bfloat16)
    matched = jnp.any(predicted[:, None, :] == actual[:, :, None], axis=2)
    missed = lax.optimization_barrier(jnp.sum(jnp.where(matched, 0.0, gates), axis=1))
    flat_true = actual.reshape(-1)
    flat_gate = gates.reshape(-1)
    capacity = N_EXPERT * (CAP + CAP_C)

    def add_expert(running, item):
        index, weight_gate, weight_up, weight_down = item
        chosen = flat_true == index
        picked = jnp.nonzero(chosen, size=capacity, fill_value=0)[0].astype(jnp.int32)
        valid = jnp.arange(capacity, dtype=jnp.int32) < jnp.sum(chosen.astype(jnp.int32))
        token_index = (picked // TOP).astype(jnp.int32)
        result = expert_rows(normed[token_index], weight_gate, weight_up, weight_down).astype(jnp.float32)
        weight = jnp.where(valid, flat_gate[picked], 0.0)
        return (running.at[token_index].add(weight[:, None] * result), None)
    mixture, _ = lax.scan(add_expert, jnp.zeros((SEQUENCE_TOKENS, D), jnp.float32), (jnp.arange(ACTIVE_EXPERTS, dtype=jnp.int32), w_gate, w_up, w_down))
    return (attended, mixture.astype(jnp.bfloat16), missed)
```

```python
import jax
import jax.numpy as jnp
from jax import lax
from jax.sharding import PartitionSpec as P

ROPE = 64
VDIM = 128
LANES = 128

EPS = 1e-06
FLOOR = -1e30


def line_send(value, axis, size, step):
    pairs = [(i, i + step) for i in range(size) if 0 <= i + step < size]
    return lax.ppermute(value, axis, pairs)


def line_gather(value, axis, size):
    me = lax.axis_index(axis)
    rights, lefts = [value], [value]
    for _ in range(1, size):
        rights.append(line_send(rights[-1], axis, size, 1))
        lefts.append(line_send(lefts[-1], axis, size, -1))
    return [value] + [jnp.where(me >= s, rights[s], lefts[size - s]) for s in range(1, size)]


def add(first, second):
    return (first.astype(jnp.float32) + second.astype(jnp.float32)).astype(first.dtype)


def line_scatter(blocks, axis, size):
    right, left = None, None
    for far in range(size - 1, 0, -1):
        out_right, out_left = blocks[size - far], blocks[far]
        if right is not None:
            out_right, out_left = add(out_right, right), add(out_left, left)
        right = line_send(out_right, axis, size, 1)
        left = line_send(out_left, axis, size, -1)
    return (
        blocks[0].astype(jnp.float32) + right.astype(jnp.float32) + left.astype(jnp.float32)
    ).astype(blocks[0].dtype)


def flip(value, axis, size, bit):
    return lax.ppermute(value, axis, [(i, i ^ bit) for i in range(size)])


def halve(value, axis, size, dim):
    me = lax.axis_index(axis)
    bit = 1
    while bit < size:
        half = value.shape[dim] // 2
        low = lax.slice_in_dim(value, 0, half, axis=dim)
        high = lax.slice_in_dim(value, half, 2 * half, axis=dim)
        mine = (me & bit) == 0
        got = flip(jnp.where(mine, high, low), axis, size, bit)
        value = jnp.where(mine, low, high).astype(jnp.float32) + got.astype(jnp.float32)
        bit *= 2
        if bit < size:
            value = value.astype(got.dtype)
    return value


def unhalve(value, axis, size, dim):
    me = lax.axis_index(axis)
    bit = size // 2
    while bit >= 1:
        got = flip(value, axis, size, bit)
        mine = (me & bit) == 0
        value = jnp.concatenate(
            [jnp.where(mine, value, got), jnp.where(mine, got, value)], axis=dim
        )
        bit //= 2
    return value


def attend(q_absorbed, kv_latent, w_values, experts):
    token_count = q_absorbed.shape[0]
    heads_here, latent_width, _ = w_values.shape
    key_width = kv_latent.shape[1]
    scale = (VDIM + ROPE) ** (-0.5)
    me = lax.axis_index("expert")
    blocks = [kv_latent]
    for _ in range(1, experts):
        blocks.append(line_send(blocks[-1], "expert", experts, 1))
    keys = jnp.concatenate(blocks, axis=0)
    queries = q_absorbed.reshape(token_count * heads_here, key_width)
    query_pos = jnp.repeat(jnp.arange(token_count, dtype=jnp.int32), heads_here)
    index = jnp.arange(keys.shape[0], dtype=jnp.int32)
    back, place = index // token_count, index % token_count
    own = (back[None, :] == 0) & (query_pos[:, None] >= place[None, :])
    visible = own | ((back >= 1) & (back <= me))[None, :]
    scores = (
        lax.dot_general(
            queries, keys, (((1,), (1,)), ((), ())), preferred_element_type=jnp.float32
        )
        * scale
    )
    masked = jnp.where(visible, scores, FLOOR)
    largest = jnp.max(masked, axis=1)
    expo = jnp.where(visible, jnp.exp(masked - largest[:, None]), 0.0)
    denominator = jnp.sum(expo, axis=1)
    accum = jnp.dot(
        expo.astype(jnp.bfloat16), keys[:, :latent_width], preferred_element_type=jnp.float32
    )
    latent = (
        (accum / denominator[:, None])
        .astype(jnp.bfloat16)
        .reshape(token_count, heads_here, latent_width)
    )
    heads_out = jnp.einsum(
        "thc,hcv->thv", latent, w_values, preferred_element_type=jnp.float32
    ).astype(jnp.bfloat16)
    return heads_out.reshape(token_count, heads_here * w_values.shape[2])


def project(heads_out, w_out, experts, tensors):
    token_count = heads_out.shape[0]
    slots = jnp.concatenate(line_gather(heads_out, "expert", experts), axis=0)
    partial = jnp.dot(slots, w_out, preferred_element_type=jnp.float32).astype(jnp.bfloat16)
    if experts == tensors:
        mine = halve(partial, "tensor", tensors, 0).astype(jnp.bfloat16)
        bits = tensors.bit_length() - 1
        pairs = []
        for e in range(experts):
            for t in range(tensors):
                slot = int(format(t, "0%db" % bits)[::-1], 2)
                pairs.append((e * tensors + t, (e - slot) % experts * tensors + e))
        return lax.ppermute(mine, ("expert", "tensor"), pairs)
    me = lax.axis_index("expert")
    order = (me - jnp.arange(experts)) % experts
    blocks = partial.reshape(experts, token_count, -1)[order].reshape(partial.shape)
    rows = lax.all_to_all(blocks, "expert", split_axis=0, concat_axis=1, tiled=True)
    return lax.psum_scatter(rows, "tensor", scatter_dimension=1, tiled=True)


def mix(layer_input, norm_gain, actual, gates, w_gate, w_up, w_down, experts, tensors):
    token_count = layer_input.shape[0]
    local, slice_width, hidden = w_gate.shape
    active = local * experts
    me = lax.axis_index("expert")
    first_col = lax.axis_index("tensor") * slice_width
    features = layer_input.astype(jnp.float32)
    inverse = lax.rsqrt(jnp.mean(features * features, axis=1, keepdims=True) + EPS)
    mine = lax.dynamic_slice_in_dim(layer_input, first_col, slice_width, 1).astype(jnp.float32)
    gain_mine = lax.dynamic_slice_in_dim(norm_gain, first_col, slice_width, 0)
    normed = (mine * inverse * gain_mine).astype(jnp.bfloat16)
    ids = jnp.arange(active, dtype=jnp.int32)
    dense = jnp.sum(
        jnp.where(actual[:, :, None] == ids[None, None, :], gates[:, :, None], 0.0), axis=1
    )
    high = dense.astype(jnp.bfloat16)
    low = (dense - high.astype(jnp.float32)).astype(jnp.bfloat16)
    width = -(-2 * active // LANES) * LANES
    filler = jnp.zeros((token_count, width - 2 * active), jnp.bfloat16)
    rows = jnp.concatenate([normed, high, low, filler], axis=1)
    slots = jnp.concatenate(line_gather(rows, "expert", experts), axis=0)
    tokens = slots[:, :slice_width]
    both = slots[:, slice_width : slice_width + 2 * active].astype(jnp.float32)
    weight = both[:, :active] + both[:, active:]
    weight = lax.dynamic_slice_in_dim(weight, me * local, local, 1)
    acts = []
    for e in range(local):
        gate_part = jnp.dot(tokens, w_gate[e], preferred_element_type=jnp.float32)
        up_part = jnp.dot(tokens, w_up[e], preferred_element_type=jnp.float32)
        pair = jnp.stack([gate_part.astype(jnp.bfloat16), up_part.astype(jnp.bfloat16)])
        share = halve(pair, "tensor", tensors, 2)
        act = jax.nn.silu(share[0]) * share[1] * weight[:, e : e + 1]
        acts.append(unhalve(act.astype(jnp.bfloat16), "tensor", tensors, 1))
    acts = jnp.concatenate(acts, axis=1)
    partial = jnp.dot(
        acts, w_down.reshape(local * hidden, -1), preferred_element_type=jnp.float32
    ).astype(jnp.bfloat16)
    blocks = partial.reshape(experts, token_count, -1)
    return line_scatter([blocks[s] for s in range(experts)], "expert", experts)


def solution(mesh):
    experts, tensors = mesh.shape["expert"], mesh.shape["tensor"]

    def body(
        q_absorbed,
        kv_latent,
        w_values,
        w_out,
        layer_input,
        norm_gain,
        predicted,
        actual,
        gates,
        w_gate,
        w_up,
        w_down,
    ):
        matched = jnp.any(predicted[:, None, :] == actual[:, :, None], axis=2)
        missed = jnp.sum(jnp.where(matched, 0.0, gates), axis=1)
        mixture = mix(
            layer_input, norm_gain, actual, gates, w_gate, w_up, w_down, experts, tensors
        )
        heads_out = attend(q_absorbed, kv_latent, w_values, experts)
        attended = project(heads_out, w_out, experts, tensors)
        return (attended, mixture, missed)

    placed = (
        P(("group", "expert"), "tensor"),
        P(("group", "expert"), None),
        P("tensor", None, None),
        P("tensor", "expert"),
        P(("group", "expert"), None),
        P(),
        P(("group", "expert"), None),
        P(("group", "expert"), None),
        P(("group", "expert"), None),
        P("expert", "tensor", None),
        P("expert", "tensor", None),
        P("expert", None, "tensor"),
    )
    return jax.shard_map(
        body,
        mesh=mesh,
        in_specs=placed,
        out_specs=(
            P(("group", "expert"), "tensor"),
            P(("group", "expert"), "tensor"),
            P(("group", "expert")),
        ),
        check_vma=False,
    )
```

```python
import functools

import jax
import jax.numpy as jnp
from jax import lax
from jax.experimental import pallas as pl
from jax.experimental.pallas import tpu as pltpu
from jax.sharding import PartitionSpec as P


GROUP, EXPERT, TENSOR = "group", "expert", "tensor"
ROPE = 64
VDIM = 128
LANES = 128

EPS = 1e-06
FLOOR = -1e30


def line_send(value, axis, size, step):
    pairs = [(i, i + step) for i in range(size) if 0 <= i + step < size]
    return lax.ppermute(value, axis, pairs)


def line_gather(value, axis, size):
    me = lax.axis_index(axis)
    rights, lefts = [value], [value]
    for _ in range(1, size):
        rights.append(line_send(rights[-1], axis, size, 1))
        lefts.append(line_send(lefts[-1], axis, size, -1))
    return [value] + [jnp.where(me >= s, rights[s], lefts[size - s]) for s in range(1, size)]


def add(first, second):
    return (first.astype(jnp.float32) + second.astype(jnp.float32)).astype(first.dtype)


def line_scatter(blocks, axis, size):
    right, left = None, None
    for far in range(size - 1, 0, -1):
        out_right, out_left = blocks[size - far], blocks[far]
        if right is not None:
            out_right, out_left = add(out_right, right), add(out_left, left)
        right = line_send(out_right, axis, size, 1)
        left = line_send(out_left, axis, size, -1)
    return (
        blocks[0].astype(jnp.float32) + right.astype(jnp.float32) + left.astype(jnp.float32)
    ).astype(blocks[0].dtype)


def flip(value, axis, size, bit):
    return lax.ppermute(value, axis, [(i, i ^ bit) for i in range(size)])


def halve(value, axis, size, dim):
    me = lax.axis_index(axis)
    bit = 1
    while bit < size:
        half = value.shape[dim] // 2
        low = lax.slice_in_dim(value, 0, half, axis=dim)
        high = lax.slice_in_dim(value, half, 2 * half, axis=dim)
        mine = (me & bit) == 0
        got = flip(jnp.where(mine, high, low), axis, size, bit)
        value = jnp.where(mine, low, high).astype(jnp.float32) + got.astype(jnp.float32)
        bit *= 2
        if bit < size:
            value = value.astype(got.dtype)
    return value


def unhalve(value, axis, size, dim):
    me = lax.axis_index(axis)
    bit = size // 2
    while bit >= 1:
        got = flip(value, axis, size, bit)
        mine = (me & bit) == 0
        value = jnp.concatenate(
            [jnp.where(mine, value, got), jnp.where(mine, got, value)], axis=dim
        )
        bit //= 2
    return value


def attend(q_absorbed, blocks, w_values):
    token_count = q_absorbed.shape[0]
    heads_here, latent_width, _ = w_values.shape
    key_width = blocks[0].shape[1]
    scale = (VDIM + ROPE) ** (-0.5)
    me = lax.axis_index(EXPERT)
    keys = jnp.concatenate(blocks, axis=0)
    queries = q_absorbed.reshape(token_count * heads_here, key_width)
    query_pos = jnp.repeat(jnp.arange(token_count, dtype=jnp.int32), heads_here)
    index = jnp.arange(keys.shape[0], dtype=jnp.int32)
    back, place = index // token_count, index % token_count
    own = (back[None, :] == 0) & (query_pos[:, None] >= place[None, :])
    visible = own | ((back >= 1) & (back <= me))[None, :]
    scores = (
        lax.dot_general(
            queries, keys, (((1,), (1,)), ((), ())), preferred_element_type=jnp.float32
        )
        * scale
    )
    masked = jnp.where(visible, scores, FLOOR)
    largest = jnp.max(masked, axis=1)
    expo = jnp.where(visible, jnp.exp(masked - largest[:, None]), 0.0)
    denominator = jnp.sum(expo, axis=1)
    accum = jnp.dot(
        expo.astype(jnp.bfloat16), keys[:, :latent_width], preferred_element_type=jnp.float32
    )
    latent = (
        (accum / denominator[:, None])
        .astype(jnp.bfloat16)
        .reshape(token_count, heads_here, latent_width)
    )
    heads_out = jnp.einsum(
        "thc,hcv->thv", latent, w_values, preferred_element_type=jnp.float32
    ).astype(jnp.bfloat16)
    return heads_out.reshape(token_count, heads_here * w_values.shape[2])


def project(heads_out, w_out, experts, tensors):
    token_count = heads_out.shape[0]
    slots = jnp.concatenate(line_gather(heads_out, EXPERT, experts), axis=0)
    partial = jnp.dot(slots, w_out, preferred_element_type=jnp.float32).astype(jnp.bfloat16)
    if experts == tensors:
        mine = halve(partial, TENSOR, tensors, 0).astype(jnp.bfloat16)
        bits = tensors.bit_length() - 1
        pairs = []
        for e in range(experts):
            for t in range(tensors):
                slot = int(format(t, "0%db" % bits)[::-1], 2)
                pairs.append((e * tensors + t, (e - slot) % experts * tensors + e))
        return lax.ppermute(mine, (EXPERT, TENSOR), pairs)
    me = lax.axis_index(EXPERT)
    order = (me - jnp.arange(experts)) % experts
    blocks = partial.reshape(experts, token_count, -1)[order].reshape(partial.shape)
    rows = lax.all_to_all(blocks, EXPERT, split_axis=0, concat_axis=1, tiled=True)
    return lax.psum_scatter(rows, TENSOR, scatter_dimension=1, tiled=True)


def expert_rows(layer_input, norm_gain, actual, gates, slice_width, active):
    token_count = layer_input.shape[0]
    first_col = lax.axis_index(TENSOR) * slice_width
    features = layer_input.astype(jnp.float32)
    inverse = lax.rsqrt(jnp.mean(features * features, axis=1, keepdims=True) + EPS)
    mine = lax.dynamic_slice_in_dim(layer_input, first_col, slice_width, 1).astype(jnp.float32)
    gain_mine = lax.dynamic_slice_in_dim(norm_gain, first_col, slice_width, 0)
    normed = (mine * inverse * gain_mine).astype(jnp.bfloat16)
    ids = jnp.arange(active, dtype=jnp.int32)
    dense = jnp.sum(
        jnp.where(actual[:, :, None] == ids[None, None, :], gates[:, :, None], 0.0), axis=1
    )
    high = dense.astype(jnp.bfloat16)
    low = (dense - high.astype(jnp.float32)).astype(jnp.bfloat16)
    width = -(-2 * active // LANES) * LANES
    filler = jnp.zeros((token_count, width - 2 * active), jnp.bfloat16)
    return jnp.concatenate([normed, high, low, filler], axis=1)


def mix(layer_input, norm_gain, actual, gates, w_gate, w_up, w_down, experts, tensors):
    token_count = layer_input.shape[0]
    local, slice_width, hidden = w_gate.shape
    active = local * experts
    me = lax.axis_index(EXPERT)
    rows = expert_rows(layer_input, norm_gain, actual, gates, slice_width, active)
    slots = jnp.concatenate(line_gather(rows, EXPERT, experts), axis=0)
    tokens = slots[:, :slice_width]
    both = slots[:, slice_width : slice_width + 2 * active].astype(jnp.float32)
    weight = both[:, :active] + both[:, active:]
    weight = lax.dynamic_slice_in_dim(weight, me * local, local, 1)
    acts = []
    for e in range(local):
        gate_part = jnp.dot(tokens, w_gate[e], preferred_element_type=jnp.float32)
        up_part = jnp.dot(tokens, w_up[e], preferred_element_type=jnp.float32)
        pair = jnp.stack([gate_part.astype(jnp.bfloat16), up_part.astype(jnp.bfloat16)])
        share = halve(pair, TENSOR, tensors, 2)
        act = jax.nn.silu(share[0]) * share[1] * weight[:, e : e + 1]
        acts.append(unhalve(act.astype(jnp.bfloat16), TENSOR, tensors, 1))
    acts = jnp.concatenate(acts, axis=1)
    partial = jnp.dot(
        acts, w_down.reshape(local * hidden, -1), preferred_element_type=jnp.float32
    ).astype(jnp.bfloat16)
    blocks = partial.reshape(experts, token_count, -1)
    return line_scatter([blocks[s] for s in range(experts)], EXPERT, experts)


def after(value, *others):
    return lax.optimization_barrier((value, others))[0]


LINE = 4
VMEM = 10 * 1024 * 1024
OUTER = [(0, 1), (1, 0), (2, 3), (3, 2)]
INNER = [(1, 2), (2, 1)]
OUTWARD = [(1, 0), (2, 3)]
INWARD = [(0, 1), (3, 2)]


def block_at(device, slot):
    far = 2 if device < 2 else 0
    inner, outer = (2, 3) if far == 2 else (1, 0)
    return (device, device ^ 1, inner, outer)[slot]


def attention_kernel(flags, q_ref, even_ref, odd_ref, values_ref, out_ref, shut, *, scale):
    rows, keys = shut.shape
    heads = values_ref.shape[0]
    latent_width = values_ref.shape[1]
    value_width = values_ref.shape[2]
    width = q_ref.shape[1] // heads
    reach = even_ref.shape[1]

    @pl.when(pl.program_id(0) == 0)
    def _():
        query = lax.broadcasted_iota(jnp.int32, (rows, keys), 0)
        key = lax.broadcasted_iota(jnp.int32, (rows, keys), 1)
        open_to = jnp.where(key < rows, query, -1)
        for slot in range(1, keys // rows):
            other = flags[3] ^ slot
            limit = jnp.where(other < flags[3], keys, -1)
            open_to = jnp.where((key >= slot * rows) & (key < (slot + 1) * rows), limit, open_to)
        shut[...] = jnp.where(key <= open_to, 0.0, FLOOR)

    even = [q_ref[:, h * width : h * width + reach] for h in range(0, heads, 2)]
    odd = [q_ref[:, (h + 1) * width - reach : (h + 1) * width] for h in range(1, heads, 2)]
    for parity, group, key_ref in ((0, even, even_ref), (1, odd, odd_ref)):
        queries = jnp.concatenate(group, axis=0)
        scores = lax.dot_general(
            queries, key_ref[...], (((1,), (1,)), ((), ())), preferred_element_type=jnp.float32
        )
        scores = (scores * scale).reshape(len(group), rows, keys) + shut[...][None]
        largest = jnp.max(scores, axis=2, keepdims=True)
        expo = jnp.exp(scores - largest)
        bottom = jnp.sum(expo, axis=2, keepdims=True)
        total = jnp.dot(
            expo.astype(jnp.bfloat16).reshape(len(group) * rows, keys),
            even_ref[:, :latent_width],
            preferred_element_type=jnp.float32,
        ).reshape(len(group), rows, latent_width)
        latent = (total / bottom).astype(jnp.bfloat16)
        for index in range(len(group)):
            head = 2 * index + parity
            out_ref[:, head * value_width : (head + 1) * value_width] = jnp.dot(
                latent[index], values_ref[head], preferred_element_type=jnp.float32
            ).astype(out_ref.dtype)


HEADS_AT_ONCE = 4


def attention(q_absorbed, blocks, w_values, flags):
    rows = q_absorbed.shape[0]
    heads, latent_width, value_width = w_values.shape
    width = q_absorbed.shape[1] // heads
    keys = jnp.concatenate(blocks, axis=0)
    count, reach = keys.shape
    odd = jnp.concatenate(
        [jnp.zeros((count, reach - width), keys.dtype), keys[:, :width]], axis=1
    )
    group = HEADS_AT_ONCE
    flops = 2 * rows * count * (width + latent_width) * heads
    flops += 2 * rows * latent_width * value_width * heads
    return pl.pallas_call(
        functools.partial(attention_kernel, scale=(VDIM + ROPE) ** (-0.5)),
        out_shape=jax.ShapeDtypeStruct((rows, heads * value_width), jnp.bfloat16),
        grid_spec=pltpu.PrefetchScalarGridSpec(
            num_scalar_prefetch=1,
            grid=(heads // group,),
            in_specs=[
                pl.BlockSpec((rows, group * width), lambda h, flags: (0, h)),
                pl.BlockSpec((count, reach), lambda h, flags: (0, 0)),
                pl.BlockSpec((count, reach), lambda h, flags: (0, 0)),
                pl.BlockSpec((group, latent_width, value_width), lambda h, flags: (h, 0, 0)),
            ],
            out_specs=pl.BlockSpec((rows, group * value_width), lambda h, flags: (0, h)),
            scratch_shapes=[pltpu.VMEM((rows, count), jnp.float32)],
        ),
        cost_estimate=pl.CostEstimate(
            flops=flops,
            bytes_accessed=2 * rows * heads * width,
            transcendentals=rows * heads * count,
        ),
        compiler_params=pltpu.CompilerParams(vmem_limit_bytes=VMEM),
        name="attention",
    )(flags, q_absorbed, keys, odd, w_values)


def key_blocks(kv_latent, first_core):
    rows, width = kv_latent.shape
    half = rows // 2
    whole = jnp.pad(kv_latent, ((0, 0), (0, -width % LANES)))
    mine = jnp.where(first_core, whole[:half], whole[half:])
    got = []
    for step in range(1, LINE):
        got.append(flip(mine, EXPERT, LINE, step))
    got = jnp.stack(got)
    other = flip(got, TENSOR, LINE, 1)
    full = jnp.concatenate(
        [jnp.where(first_core, got, other), jnp.where(first_core, other, got)], axis=1
    )
    return [whole] + [full[index] for index in range(LINE - 1)]


def rows_kernel(flags, *refs, parts, rows, first):
    part_refs, (gate_ref, up_ref, send_ref, keep_ref, tokens) = refs[:parts], refs[parts:]
    item, side = pl.program_id(0), pl.program_id(1)

    @pl.when((item == 0) & (side == 0))
    def _():
        if parts == 2:
            tokens[:rows] = part_refs[0][...]
            tokens[rows:] = part_refs[1][...]
        else:

            @pl.when(flags[2] == 1)
            def _():
                tokens[:rows] = part_refs[0][...]
                tokens[rows:] = part_refs[1][...]

            @pl.when(flags[2] == 0)
            def _():
                tokens[:rows] = part_refs[2][...]
                tokens[rows:] = part_refs[3][...]

    def both(out_ref, core):
        half = gate_ref.shape[2] // 2
        span = pl.ds(pl.multiple_of(core * half, half), half)
        for index, weight_ref in enumerate((gate_ref, up_ref)):
            out_ref[index, 0] = jnp.dot(
                tokens[...], weight_ref[first + item, :, span], preferred_element_type=jnp.float32
            ).astype(out_ref.dtype)

    @pl.when(side == 0)
    def _():
        both(send_ref, 1 - flags[0])

    @pl.when(side == 1)
    def _():
        both(keep_ref, flags[0])


def stage_kernel(*refs):
    half = len(refs) // 2
    sources, targets, sems = refs[:half], refs[half : 2 * half], refs[-1]
    copies = []
    for which in range(half):
        for item in range(sources[which].shape[0]):
            copies.append(
                pltpu.make_async_copy(
                    sources[which].at[item], targets[which].at[item], sems.at[which, item]
                )
            )
    for copy in copies:
        copy.start()
    for copy in copies:
        copy.wait()


def stage(*weights):
    return pl.pallas_call(
        stage_kernel,
        out_shape=tuple(pltpu.VMEM(weight.shape, weight.dtype) for weight in weights),
        in_specs=[pl.BlockSpec(memory_space=pltpu.HBM)] * len(weights),
        out_specs=(pl.BlockSpec(memory_space=pltpu.VMEM),) * len(weights),
        scratch_shapes=[pltpu.SemaphoreType.DMA((len(weights), weights[0].shape[0]))],
        cost_estimate=pl.CostEstimate(
            flops=0, bytes_accessed=2 * sum(weight.size for weight in weights), transcendentals=0
        ),
        compiler_params=pltpu.CompilerParams(vmem_limit_bytes=1024 * 1024),
        name="stage",
    )(*weights)


def gate_up(parts, flags, w_gate, w_up, first, count):
    rows = parts[0].shape[0]
    _, depth, hidden = w_gate.shape
    half = hidden // 2
    out_spec = pl.BlockSpec((2, 1, 2 * rows, half), lambda e, j, flags: (0, e, 0, 0))
    out = jax.ShapeDtypeStruct((2, count, 2 * rows, half), jnp.bfloat16)
    return pl.pallas_call(
        functools.partial(rows_kernel, parts=len(parts), rows=rows, first=first),
        out_shape=(out, out),
        grid_spec=pltpu.PrefetchScalarGridSpec(
            num_scalar_prefetch=1,
            grid=(count, 2),
            in_specs=[pl.BlockSpec((rows, depth), lambda e, j, flags: (0, 0))] * len(parts)
            + [pl.BlockSpec(memory_space=pltpu.VMEM)] * 2,
            out_specs=(out_spec, out_spec),
            scratch_shapes=[pltpu.VMEM((2 * rows, depth), jnp.bfloat16)],
        ),
        cost_estimate=pl.CostEstimate(
            flops=8 * rows * depth * hidden * count,
            bytes_accessed=4 * depth * hidden * count,
            transcendentals=0,
        ),
        compiler_params=pltpu.CompilerParams(vmem_limit_bytes=VMEM),
        name="gate_up",
    )(flags, *parts, w_gate, w_up)


def down_kernel(flags, *refs, counts, rows):
    pieces, (weight_ref, low_ref, high_ref, acts) = refs[: 2 * len(counts)], refs[2 * len(counts) :]
    quarter = pieces[0].shape[3]

    @pl.when(pl.program_id(0) == 0)
    def _():
        first = 0
        for index, count in enumerate(counts):
            for item in range(count):
                for core in range(2):
                    for chip in range(2):
                        column = (first + item) * 4 + 2 * core + chip
                        span = slice(column * quarter, (column + 1) * quarter)
                        here, there = pieces[2 * index], pieces[2 * index + 1]
                        slot = flags[1] if chip == 0 else 1 - flags[1]

                        @pl.when(flags[0] == core)
                        def _(here=here, span=span, slot=slot, item=item):
                            acts[:, span] = here[slot, item]

                        @pl.when(flags[0] != core)
                        def _(there=there, span=span, slot=slot, item=item):
                            acts[:, span] = there[slot, item]

            first += count

    depth = weight_ref.shape[0] * weight_ref.shape[1]
    tile = low_ref.shape[1]
    span = pl.ds(pl.multiple_of(pl.program_id(0) * tile, tile), tile)
    total = jnp.dot(
        acts[...],
        weight_ref[:, :, span].reshape(depth, tile),
        preferred_element_type=jnp.float32,
    )
    low_ref[...] = total[:rows].astype(low_ref.dtype)
    high_ref[...] = total[rows:].astype(high_ref.dtype)


def down(pieces, flags, w_down):
    counts = [here.shape[1] for here, _ in pieces]
    _, _, rows, _ = pieces[0][0].shape
    experts, hidden, width = w_down.shape
    tile = 2 * LANES if width % (2 * LANES) == 0 else LANES
    flat = [array for pair in pieces for array in pair]
    out = jax.ShapeDtypeStruct((rows // 2, width), jnp.bfloat16)
    return pl.pallas_call(
        functools.partial(down_kernel, counts=counts, rows=rows // 2),
        out_shape=(out, out),
        grid_spec=pltpu.PrefetchScalarGridSpec(
            num_scalar_prefetch=1,
            grid=(width // tile,),
            in_specs=[pl.BlockSpec(array.shape, lambda n, flags: (0, 0, 0, 0)) for array in flat]
            + [pl.BlockSpec(memory_space=pltpu.VMEM)],
            out_specs=[pl.BlockSpec((rows // 2, tile), lambda n, flags: (0, n))] * 2,
            scratch_shapes=[pltpu.VMEM((rows, experts * hidden), jnp.bfloat16)],
        ),
        cost_estimate=pl.CostEstimate(
            flops=2 * rows * hidden * width * experts,
            bytes_accessed=2 * hidden * width * experts,
            transcendentals=0,
        ),
        compiler_params=pltpu.CompilerParams(vmem_limit_bytes=VMEM),
        name="down",
    )(flags, *flat, w_down)


def merge_kernel(flags, keep_ref, got_ref, out_ref, kept_ref):
    quarter = out_ref.shape[3]

    def part(chip):
        span = pl.ds(pl.multiple_of(chip * quarter, quarter), quarter)
        here = keep_ref[:, :, :, span].astype(jnp.float32)
        return here + got_ref[:, :, :, span].astype(jnp.float32)

    out_ref[...] = part(1 - flags[1]).astype(out_ref.dtype)
    kept_ref[...] = part(flags[1])


def core_sum(send, keep, flags):
    got = flip(send, TENSOR, LINE, 1)
    kinds, count, rows, half = keep.shape
    shape = (kinds, count, rows, half // 2)
    spec = pl.BlockSpec((kinds, 1, rows, half), lambda e, flags: (0, e, 0, 0))
    out_spec = pl.BlockSpec((kinds, 1, rows, half // 2), lambda e, flags: (0, e, 0, 0))
    return pl.pallas_call(
        merge_kernel,
        out_shape=(
            jax.ShapeDtypeStruct(shape, jnp.bfloat16),
            jax.ShapeDtypeStruct(shape, jnp.float32),
        ),
        grid_spec=pltpu.PrefetchScalarGridSpec(
            num_scalar_prefetch=1, grid=(count,), in_specs=[spec] * 2, out_specs=(out_spec,) * 2
        ),
        cost_estimate=pl.CostEstimate(
            flops=keep.size, bytes_accessed=7 * keep.size, transcendentals=0
        ),
        compiler_params=pltpu.CompilerParams(vmem_limit_bytes=VMEM),
        name="merge",
    )(flags, keep, got)


def activate_kernel(flags, kept_ref, got_ref, *refs, first, local, active):
    gate_refs, act_ref = refs[:-1], refs[-1]
    rows = gate_refs[0].shape[0]
    which = flags[3] * local + first + pl.program_id(0)
    lane = lax.broadcasted_iota(jnp.int32, gate_refs[0].shape, 1)
    mine = (lane == which) | (lane == which + active)

    def weight(index):
        block = gate_refs[index][...]
        if len(gate_refs) > 2:
            block = jnp.where(flags[2] == 1, block, gate_refs[index + 2][...])
        return jnp.sum(jnp.where(mine, block.astype(jnp.float32), 0.0), axis=1, keepdims=True)

    for index in range(2):
        span = slice(index * rows, (index + 1) * rows)
        gate = kept_ref[0, 0, span] + got_ref[0, 0, span].astype(jnp.float32)
        up = kept_ref[1, 0, span] + got_ref[1, 0, span].astype(jnp.float32)
        act_ref[0, span] = (jax.nn.silu(gate) * up * weight(index)).astype(act_ref.dtype)


def activate(kept, got, parts, flags, first, local, depth):
    kinds, count, rows, quarter = kept.shape
    spec = pl.BlockSpec((kinds, 1, rows, quarter), lambda e, flags: (0, e, 0, 0))
    gate_spec = pl.BlockSpec((rows // 2, LANES), lambda e, flags: (0, depth // LANES))
    return pl.pallas_call(
        functools.partial(activate_kernel, first=first, local=local, active=local * LINE),
        out_shape=jax.ShapeDtypeStruct((count, rows, quarter), jnp.bfloat16),
        grid_spec=pltpu.PrefetchScalarGridSpec(
            num_scalar_prefetch=1,
            grid=(count,),
            in_specs=[spec] * 2 + [gate_spec] * len(parts),
            out_specs=pl.BlockSpec((1, rows, quarter), lambda e, flags: (e, 0, 0)),
        ),
        cost_estimate=pl.CostEstimate(
            flops=4 * kept.size, bytes_accessed=7 * kept.size, transcendentals=kept.size
        ),
        compiler_params=pltpu.CompilerParams(vmem_limit_bytes=VMEM),
        name="activate",
    )(flags, kept, got, *parts)


def spread(act, chip):
    here = jnp.stack([act, chip])
    return here, flip(here, TENSOR, 4, 1)


def layer(
    q_absorbed,
    kv_latent,
    w_values,
    w_out,
    layer_input,
    norm_gain,
    actual,
    gates,
    w_gate,
    w_up,
    w_down,
):
    local, slice_width, _ = w_gate.shape
    me, side = lax.axis_index(EXPERT), lax.axis_index(TENSOR)
    inner = (me == 1) | (me == 2)
    flags = jnp.stack([side & 1, side >> 1, inner.astype(jnp.int32), me.astype(jnp.int32)])
    inner, first_core, flags = lax.optimization_barrier((inner, (side & 1) == 0, flags))
    own = expert_rows(layer_input, norm_gain, actual, gates, slice_width, local * LINE)
    pair = lax.ppermute(own, EXPERT, OUTER)
    across = lax.ppermute(own, EXPERT, INNER)
    blocks = key_blocks(after(kv_latent, own), first_core)
    gate_near, up_near = stage(*after((w_gate, w_up), own, flags))
    pair, across, gate_near = after((pair, across, gate_near), gate_near)
    beyond = lax.ppermute(pair, EXPERT, INNER)
    out_first = lax.ppermute(across, EXPERT, OUTWARD)

    step = local // 2

    def turn(parts, index):
        send, keep = gate_up(parts, flags, gate_near, up_near, index % 2 * step, step)
        out, kept = core_sum(send, keep, flags)
        return out, kept, flip(out, TENSOR, 4, 2)

    def act(kept, got, parts, first):
        return activate(kept, got, parts, flags, first, local, slice_width)

    def spread_chip(acts):
        return flip(acts, TENSOR, 4, 2)

    out0, kept0, got0 = turn([own, pair], 0)
    out_second = lax.ppermute(beyond, EXPERT, OUTWARD)
    near_own, near_pair = after((own, pair), out0, beyond)
    out1, kept1, got1 = turn([near_own, near_pair], 1)
    near = [near_own, near_pair]
    blocks = after(blocks, out1)
    heads_out = attention(q_absorbed, blocks, w_values, flags)
    across, beyond, out_first, out_second = after(
        (across, beyond, out_first, out_second), heads_out
    )
    far = [across, beyond, out_first, out_second]
    pair_heads = lax.ppermute(heads_out, EXPERT, OUTER)
    across_heads = lax.ppermute(heads_out, EXPERT, INNER)
    out2, kept2, got2 = turn(far, 2)
    pair_heads, across_heads, far = after((pair_heads, across_heads, far), out2)
    beyond_heads = lax.ppermute(pair_heads, EXPERT, INNER)
    first_heads = lax.ppermute(across_heads, EXPERT, OUTWARD)
    out3, kept3, got3 = turn(far, 3)
    beyond_heads, got2, far = after((beyond_heads, got2, far), out3)
    second_heads = lax.ppermute(beyond_heads, EXPERT, OUTWARD)
    act2 = act(kept2, got2, far, 0)
    chip2 = spread_chip(act2)
    got0, got1 = after((got0, got1), act2)
    act0 = act(kept0, got0, near, 0)
    act1 = act(kept1, got1, near, step)
    (down_near,) = stage(after(w_down, act0, act1))
    got3 = after(got3, down_near)
    act3 = act(kept3, got3, far, step)
    chip3 = spread_chip(act3)
    act0, act1 = after((act0, act1), act3)
    chip0 = spread_chip(act0)
    chip1 = spread_chip(act1)
    first_heads, second_heads, beyond_heads = after(
        (first_heads, second_heads, beyond_heads), act3
    )
    slots = jnp.concatenate(
        [
            heads_out,
            pair_heads,
            jnp.where(inner, across_heads, first_heads),
            jnp.where(inner, beyond_heads, second_heads),
        ],
        axis=0,
    )
    partial = jnp.dot(slots, w_out, preferred_element_type=jnp.float32).astype(jnp.bfloat16)
    chip2, chip3 = after((chip2, chip3), partial)
    far_pieces = [spread(act2, chip2), spread(act3, chip3)]
    far_first, far_second = down(far_pieces, flags, down_near)
    in_second = lax.ppermute(far_second, EXPERT, INWARD)
    in_first = lax.ppermute(far_first, EXPERT, INWARD)
    partial, chip0, chip1 = after((partial, chip0, chip1), far_first)
    near_pieces = [spread(act0, chip0), spread(act1, chip1)]
    near_own, near_pair = down(near_pieces, flags, down_near)
    got_second = lax.ppermute(add(far_second, in_second), EXPERT, INNER)
    got_first = lax.ppermute(add(far_first, in_first), EXPERT, INNER)
    got_pair = lax.ppermute(add(near_pair, got_second), EXPERT, OUTER)
    mixture = (
        near_own.astype(jnp.float32) + got_first.astype(jnp.float32) + got_pair.astype(jnp.float32)
    ).astype(jnp.bfloat16)
    mine = halve(partial, TENSOR, 4, 0).astype(jnp.bfloat16)
    pairs = []
    for e in range(LINE):
        for t in range(LINE):
            slot = 2 * (t & 1) + (t >> 1)
            pairs.append((e * LINE + t, block_at(e, slot) * LINE + e))
    attended = lax.ppermute(mine, (EXPERT, TENSOR), pairs)
    return attended, mixture


def solution(mesh):
    experts, tensors = mesh.shape[EXPERT], mesh.shape[TENSOR]

    def body(
        q_absorbed,
        kv_latent,
        w_values,
        w_out,
        layer_input,
        norm_gain,
        predicted,
        actual,
        gates,
        w_gate,
        w_up,
        w_down,
    ):
        matched = jnp.any(predicted[:, None, :] == actual[:, :, None], axis=2)
        missed = jnp.sum(jnp.where(matched, 0.0, gates), axis=1)
        if experts == LINE and tensors == LINE:
            attended, mixture = layer(
                q_absorbed,
                kv_latent,
                w_values,
                w_out,
                layer_input,
                norm_gain,
                actual,
                gates,
                w_gate,
                w_up,
                w_down,
            )
            return (attended, mixture, missed)
        mixture = mix(
            layer_input, norm_gain, actual, gates, w_gate, w_up, w_down, experts, tensors
        )
        blocks = [kv_latent]
        for _ in range(1, experts):
            blocks.append(line_send(blocks[-1], EXPERT, experts, 1))
        heads_out = attend(q_absorbed, blocks, w_values)
        attended = project(heads_out, w_out, experts, tensors)
        return (attended, mixture, missed)

    placed = (
        P((GROUP, EXPERT), TENSOR),
        P((GROUP, EXPERT), None),
        P(TENSOR, None, None),
        P(TENSOR, EXPERT),
        P((GROUP, EXPERT), None),
        P(),
        P((GROUP, EXPERT), None),
        P((GROUP, EXPERT), None),
        P((GROUP, EXPERT), None),
        P(EXPERT, TENSOR, None),
        P(EXPERT, TENSOR, None),
        P(EXPERT, None, TENSOR),
    )
    return jax.shard_map(
        body,
        mesh=mesh,
        in_specs=placed,
        out_specs=(
            P((GROUP, EXPERT), TENSOR),
            P((GROUP, EXPERT), TENSOR),
            P((GROUP, EXPERT)),
        ),
        check_vma=False,
    )
```

```python
import functools

import jax
import jax.numpy as jnp
from jax import lax
from jax.experimental import pallas as pl
from jax.experimental.pallas import tpu as pltpu
from jax.sharding import PartitionSpec as P


GROUP, EXPERT, TENSOR = "group", "expert", "tensor"
ROPE = 64
VDIM = 128
LANES = 128

EPS = 1e-06
FLOOR = -1e30


def line_send(value, axis, size, step):
    pairs = [(i, i + step) for i in range(size) if 0 <= i + step < size]
    return lax.ppermute(value, axis, pairs)


def line_gather(value, axis, size):
    me = lax.axis_index(axis)
    rights, lefts = [value], [value]
    for _ in range(1, size):
        rights.append(line_send(rights[-1], axis, size, 1))
        lefts.append(line_send(lefts[-1], axis, size, -1))
    return [value] + [jnp.where(me >= s, rights[s], lefts[size - s]) for s in range(1, size)]


def add(first, second):
    return (first.astype(jnp.float32) + second.astype(jnp.float32)).astype(first.dtype)


def line_scatter(blocks, axis, size):
    right, left = None, None
    for far in range(size - 1, 0, -1):
        out_right, out_left = blocks[size - far], blocks[far]
        if right is not None:
            out_right, out_left = add(out_right, right), add(out_left, left)
        right = line_send(out_right, axis, size, 1)
        left = line_send(out_left, axis, size, -1)
    return (
        blocks[0].astype(jnp.float32) + right.astype(jnp.float32) + left.astype(jnp.float32)
    ).astype(blocks[0].dtype)


def flip(value, axis, size, bit):
    return lax.ppermute(value, axis, [(i, i ^ bit) for i in range(size)])


def halve(value, axis, size, dim):
    me = lax.axis_index(axis)
    bit = 1
    while bit < size:
        half = value.shape[dim] // 2
        low = lax.slice_in_dim(value, 0, half, axis=dim)
        high = lax.slice_in_dim(value, half, 2 * half, axis=dim)
        mine = (me & bit) == 0
        got = flip(jnp.where(mine, high, low), axis, size, bit)
        value = jnp.where(mine, low, high).astype(jnp.float32) + got.astype(jnp.float32)
        bit *= 2
        if bit < size:
            value = value.astype(got.dtype)
    return value


def unhalve(value, axis, size, dim):
    me = lax.axis_index(axis)
    bit = size // 2
    while bit >= 1:
        got = flip(value, axis, size, bit)
        mine = (me & bit) == 0
        value = jnp.concatenate(
            [jnp.where(mine, value, got), jnp.where(mine, got, value)], axis=dim
        )
        bit //= 2
    return value


def attend(q_absorbed, blocks, w_values):
    token_count = q_absorbed.shape[0]
    heads_here, latent_width, _ = w_values.shape
    key_width = blocks[0].shape[1]
    scale = (VDIM + ROPE) ** (-0.5)
    me = lax.axis_index(EXPERT)
    keys = jnp.concatenate(blocks, axis=0)
    queries = q_absorbed.reshape(token_count * heads_here, key_width)
    query_pos = jnp.repeat(jnp.arange(token_count, dtype=jnp.int32), heads_here)
    index = jnp.arange(keys.shape[0], dtype=jnp.int32)
    back, place = index // token_count, index % token_count
    own = (back[None, :] == 0) & (query_pos[:, None] >= place[None, :])
    visible = own | ((back >= 1) & (back <= me))[None, :]
    scores = (
        lax.dot_general(
            queries, keys, (((1,), (1,)), ((), ())), preferred_element_type=jnp.float32
        )
        * scale
    )
    masked = jnp.where(visible, scores, FLOOR)
    largest = jnp.max(masked, axis=1)
    expo = jnp.where(visible, jnp.exp(masked - largest[:, None]), 0.0)
    denominator = jnp.sum(expo, axis=1)
    accum = jnp.dot(
        expo.astype(jnp.bfloat16), keys[:, :latent_width], preferred_element_type=jnp.float32
    )
    latent = (
        (accum / denominator[:, None])
        .astype(jnp.bfloat16)
        .reshape(token_count, heads_here, latent_width)
    )
    heads_out = jnp.einsum(
        "thc,hcv->thv", latent, w_values, preferred_element_type=jnp.float32
    ).astype(jnp.bfloat16)
    return heads_out.reshape(token_count, heads_here * w_values.shape[2])


def project(heads_out, w_out, experts, tensors):
    token_count = heads_out.shape[0]
    slots = jnp.concatenate(line_gather(heads_out, EXPERT, experts), axis=0)
    partial = jnp.dot(slots, w_out, preferred_element_type=jnp.float32).astype(jnp.bfloat16)
    if experts == tensors:
        mine = halve(partial, TENSOR, tensors, 0).astype(jnp.bfloat16)
        bits = tensors.bit_length() - 1
        pairs = []
        for e in range(experts):
            for t in range(tensors):
                slot = int(format(t, "0%db" % bits)[::-1], 2)
                pairs.append((e * tensors + t, (e - slot) % experts * tensors + e))
        return lax.ppermute(mine, (EXPERT, TENSOR), pairs)
    me = lax.axis_index(EXPERT)
    order = (me - jnp.arange(experts)) % experts
    blocks = partial.reshape(experts, token_count, -1)[order].reshape(partial.shape)
    rows = lax.all_to_all(blocks, EXPERT, split_axis=0, concat_axis=1, tiled=True)
    return lax.psum_scatter(rows, TENSOR, scatter_dimension=1, tiled=True)


def expert_rows(layer_input, norm_gain, actual, gates, slice_width, active):
    token_count = layer_input.shape[0]
    first_col = lax.axis_index(TENSOR) * slice_width
    features = layer_input.astype(jnp.float32)
    inverse = lax.rsqrt(jnp.mean(features * features, axis=1, keepdims=True) + EPS)
    mine = lax.dynamic_slice_in_dim(layer_input, first_col, slice_width, 1).astype(jnp.float32)
    gain_mine = lax.dynamic_slice_in_dim(norm_gain, first_col, slice_width, 0)
    normed = (mine * inverse * gain_mine).astype(jnp.bfloat16)
    ids = jnp.arange(active, dtype=jnp.int32)
    dense = jnp.sum(
        jnp.where(actual[:, :, None] == ids[None, None, :], gates[:, :, None], 0.0), axis=1
    )
    high = dense.astype(jnp.bfloat16)
    low = (dense - high.astype(jnp.float32)).astype(jnp.bfloat16)
    width = -(-2 * active // LANES) * LANES
    filler = jnp.zeros((token_count, width - 2 * active), jnp.bfloat16)
    return jnp.concatenate([normed, high, low, filler], axis=1)


def mix(layer_input, norm_gain, actual, gates, w_gate, w_up, w_down, experts, tensors):
    token_count = layer_input.shape[0]
    local, slice_width, hidden = w_gate.shape
    active = local * experts
    me = lax.axis_index(EXPERT)
    rows = expert_rows(layer_input, norm_gain, actual, gates, slice_width, active)
    slots = jnp.concatenate(line_gather(rows, EXPERT, experts), axis=0)
    tokens = slots[:, :slice_width]
    both = slots[:, slice_width : slice_width + 2 * active].astype(jnp.float32)
    weight = both[:, :active] + both[:, active:]
    weight = lax.dynamic_slice_in_dim(weight, me * local, local, 1)
    acts = []
    for e in range(local):
        gate_part = jnp.dot(tokens, w_gate[e], preferred_element_type=jnp.float32)
        up_part = jnp.dot(tokens, w_up[e], preferred_element_type=jnp.float32)
        pair = jnp.stack([gate_part.astype(jnp.bfloat16), up_part.astype(jnp.bfloat16)])
        share = halve(pair, TENSOR, tensors, 2)
        act = jax.nn.silu(share[0]) * share[1] * weight[:, e : e + 1]
        acts.append(unhalve(act.astype(jnp.bfloat16), TENSOR, tensors, 1))
    acts = jnp.concatenate(acts, axis=1)
    partial = jnp.dot(
        acts, w_down.reshape(local * hidden, -1), preferred_element_type=jnp.float32
    ).astype(jnp.bfloat16)
    blocks = partial.reshape(experts, token_count, -1)
    return line_scatter([blocks[s] for s in range(experts)], EXPERT, experts)


def after(value, *others):
    return lax.optimization_barrier((value, others))[0]


LINE = 4
VMEM = 10 * 1024 * 1024
STAGE_VMEM = 30 * 1024 * 1024
OUTER = [(0, 1), (1, 0), (2, 3), (3, 2)]
INNER = [(1, 2), (2, 1)]
OUTWARD = [(1, 0), (2, 3)]
INWARD = [(0, 1), (3, 2)]


def block_at(device, slot):
    far = 2 if device < 2 else 0
    inner, outer = (2, 3) if far == 2 else (1, 0)
    return (device, device ^ 1, inner, outer)[slot]


def attention_kernel(flags, q_ref, even_ref, odd_ref, values_ref, out_ref, shut, *, scale):
    rows, keys = shut.shape
    heads = values_ref.shape[0]
    latent_width = values_ref.shape[1]
    value_width = values_ref.shape[2]
    width = q_ref.shape[1] // heads
    reach = even_ref.shape[1]

    @pl.when(pl.program_id(0) == 0)
    def _():
        query = lax.broadcasted_iota(jnp.int32, (rows, keys), 0)
        key = lax.broadcasted_iota(jnp.int32, (rows, keys), 1)
        open_to = jnp.where(key < rows, query, -1)
        for slot in range(1, keys // rows):
            other = flags[3] ^ slot
            limit = jnp.where(other < flags[3], keys, -1)
            open_to = jnp.where((key >= slot * rows) & (key < (slot + 1) * rows), limit, open_to)
        shut[...] = jnp.where(key <= open_to, 0.0, FLOOR)

    even = [q_ref[:, h * width : h * width + reach] for h in range(0, heads, 2)]
    odd = [q_ref[:, (h + 1) * width - reach : (h + 1) * width] for h in range(1, heads, 2)]
    for parity, group, key_ref in ((0, even, even_ref), (1, odd, odd_ref)):
        queries = jnp.concatenate(group, axis=0)
        scores = lax.dot_general(
            queries, key_ref[...], (((1,), (1,)), ((), ())), preferred_element_type=jnp.float32
        )
        scores = (scores * scale).reshape(len(group), rows, keys) + shut[...][None]
        largest = jnp.max(scores, axis=2, keepdims=True)
        expo = jnp.exp(scores - largest)
        bottom = jnp.sum(expo, axis=2, keepdims=True)
        total = jnp.dot(
            expo.astype(jnp.bfloat16).reshape(len(group) * rows, keys),
            even_ref[:, :latent_width],
            preferred_element_type=jnp.float32,
        ).reshape(len(group), rows, latent_width)
        latent = (total / bottom).astype(jnp.bfloat16)
        for index in range(len(group)):
            head = 2 * index + parity
            out_ref[:, head * value_width : (head + 1) * value_width] = jnp.dot(
                latent[index], values_ref[head], preferred_element_type=jnp.float32
            ).astype(out_ref.dtype)


HEADS_AT_ONCE = 4


def attention(q_absorbed, blocks, w_values, flags):
    rows = q_absorbed.shape[0]
    heads, latent_width, value_width = w_values.shape
    width = q_absorbed.shape[1] // heads
    keys = jnp.concatenate(blocks, axis=0)
    count, reach = keys.shape
    odd = jnp.concatenate(
        [jnp.zeros((count, reach - width), keys.dtype), keys[:, :width]], axis=1
    )
    group = HEADS_AT_ONCE
    flops = 2 * rows * count * (width + latent_width) * heads
    flops += 2 * rows * latent_width * value_width * heads
    return pl.pallas_call(
        functools.partial(attention_kernel, scale=(VDIM + ROPE) ** (-0.5)),
        out_shape=jax.ShapeDtypeStruct((rows, heads * value_width), jnp.bfloat16),
        grid_spec=pltpu.PrefetchScalarGridSpec(
            num_scalar_prefetch=1,
            grid=(heads // group,),
            in_specs=[
                pl.BlockSpec((rows, group * width), lambda h, flags: (0, h)),
                pl.BlockSpec((count, reach), lambda h, flags: (0, 0)),
                pl.BlockSpec((count, reach), lambda h, flags: (0, 0)),
                pl.BlockSpec((group, latent_width, value_width), lambda h, flags: (h, 0, 0)),
            ],
            out_specs=pl.BlockSpec((rows, group * value_width), lambda h, flags: (0, h)),
            scratch_shapes=[pltpu.VMEM((rows, count), jnp.float32)],
        ),
        cost_estimate=pl.CostEstimate(
            flops=flops,
            bytes_accessed=2 * rows * heads * width,
            transcendentals=rows * heads * count,
        ),
        compiler_params=pltpu.CompilerParams(vmem_limit_bytes=VMEM),
        name="attention",
    )(flags, q_absorbed, keys, odd, w_values)


def key_halves(kv_latent, first_core):
    rows, width = kv_latent.shape
    half = rows // 2
    whole = jnp.pad(kv_latent, ((0, 0), (0, -width % LANES)))
    mine = jnp.where(first_core, whole[:half], whole[half:])
    pair = flip(mine, EXPERT, LINE, 1)
    others = flip(jnp.stack([mine, pair]), EXPERT, LINE, 2)
    return whole, jnp.concatenate([pair[None], others])


def key_blocks(whole, got, first_core):
    other = flip(got, TENSOR, LINE, 1)
    full = jnp.concatenate(
        [jnp.where(first_core, got, other), jnp.where(first_core, other, got)], axis=1
    )
    return [whole] + [full[index] for index in range(LINE - 1)]


def rows_kernel(flags, *refs, parts, rows, side):
    part_refs, (gate_ref, up_ref, out_ref, tokens) = refs[:parts], refs[parts:]
    item = pl.program_id(0)

    @pl.when(item == 0)
    def _():
        if parts == 2:
            tokens[:rows] = part_refs[0][...]
            tokens[rows:] = part_refs[1][...]
        else:

            @pl.when(flags[2] == 1)
            def _():
                tokens[:rows] = part_refs[0][...]
                tokens[rows:] = part_refs[1][...]

            @pl.when(flags[2] == 0)
            def _():
                tokens[:rows] = part_refs[2][...]
                tokens[rows:] = part_refs[3][...]

    half = gate_ref.shape[2] // 2
    core = flags[0] if side else 1 - flags[0]
    span = pl.ds(pl.multiple_of(core * half, half), half)
    for index, weight_ref in enumerate((gate_ref, up_ref)):
        out_ref[index, 0] = jnp.dot(
            tokens[...], weight_ref[item, :, span], preferred_element_type=jnp.float32
        ).astype(out_ref.dtype)


def stage_kernel(*refs, first, count):
    half = len(refs) // 2
    sources, targets, sems = refs[:half], refs[half : 2 * half], refs[-1]
    copies = [
        pltpu.make_async_copy(
            sources[which].at[first + item], targets[which].at[item], sems.at[which, item]
        )
        for item in range(count)
        for which in range(half)
    ]
    for copy in copies:
        copy.start()
    for copy in copies:
        copy.wait()


def stage(weights, first, count):
    shapes = [(count,) + weight.shape[1:] for weight in weights]
    size = sum(weight[0].size * count for weight in weights)
    return pl.pallas_call(
        functools.partial(stage_kernel, first=first, count=count),
        out_shape=tuple(pltpu.VMEM(shape, weights[0].dtype) for shape in shapes),
        in_specs=[pl.BlockSpec(memory_space=pltpu.HBM)] * len(weights),
        out_specs=(pl.BlockSpec(memory_space=pltpu.VMEM),) * len(weights),
        scratch_shapes=[pltpu.SemaphoreType.DMA((len(weights), count))],
        cost_estimate=pl.CostEstimate(flops=0, bytes_accessed=2 * size, transcendentals=0),
        compiler_params=pltpu.CompilerParams(vmem_limit_bytes=STAGE_VMEM),
        name="stage",
    )(*weights)


def gate_up(parts, flags, w_gate, w_up, side):
    rows = parts[0].shape[0]
    count, depth, hidden = w_gate.shape
    half = hidden // 2
    return pl.pallas_call(
        functools.partial(rows_kernel, parts=len(parts), rows=rows, side=side),
        out_shape=jax.ShapeDtypeStruct((2, count, 2 * rows, half), jnp.bfloat16),
        grid_spec=pltpu.PrefetchScalarGridSpec(
            num_scalar_prefetch=1,
            grid=(count,),
            in_specs=[pl.BlockSpec((rows, depth), lambda e, flags: (0, 0))] * len(parts)
            + [pl.BlockSpec(memory_space=pltpu.VMEM)] * 2,
            out_specs=pl.BlockSpec((2, 1, 2 * rows, half), lambda e, flags: (0, e, 0, 0)),
            scratch_shapes=[pltpu.VMEM((2 * rows, depth), jnp.bfloat16)],
        ),
        cost_estimate=pl.CostEstimate(
            flops=4 * rows * depth * hidden * count,
            bytes_accessed=2 * depth * hidden * count,
            transcendentals=0,
        ),
        compiler_params=pltpu.CompilerParams(vmem_limit_bytes=VMEM),
        name="gate_up",
    )(flags, *parts, w_gate, w_up)


def down_kernel(flags, *refs, counts, rows):
    pieces, (weight_ref, low_ref, high_ref, acts) = refs[: 2 * len(counts)], refs[2 * len(counts) :]
    quarter = pieces[0].shape[3]

    @pl.when(pl.program_id(0) == 0)
    def _():
        first = 0
        for index, count in enumerate(counts):
            for item in range(count):
                for core in range(2):
                    for chip in range(2):
                        column = (first + item) * 4 + 2 * core + chip
                        span = slice(column * quarter, (column + 1) * quarter)
                        here, there = pieces[2 * index], pieces[2 * index + 1]
                        slot = flags[1] if chip == 0 else 1 - flags[1]

                        @pl.when(flags[0] == core)
                        def _(here=here, span=span, slot=slot, item=item):
                            acts[:, span] = here[slot, item]

                        @pl.when(flags[0] != core)
                        def _(there=there, span=span, slot=slot, item=item):
                            acts[:, span] = there[slot, item]

            first += count

    depth = weight_ref.shape[0] * weight_ref.shape[1]
    tile = low_ref.shape[1]
    span = pl.ds(pl.multiple_of(pl.program_id(0) * tile, tile), tile)
    total = jnp.dot(
        acts[...],
        weight_ref[:, :, span].reshape(depth, tile),
        preferred_element_type=jnp.float32,
    )
    low_ref[...] = total[:rows].astype(low_ref.dtype)
    high_ref[...] = total[rows:].astype(high_ref.dtype)


def down(pieces, flags, w_down):
    counts = [here.shape[1] for here, _ in pieces]
    _, _, rows, _ = pieces[0][0].shape
    experts, hidden, width = w_down.shape
    tile = 2 * LANES if width % (2 * LANES) == 0 else LANES
    flat = [array for pair in pieces for array in pair]
    out = jax.ShapeDtypeStruct((rows // 2, width), jnp.bfloat16)
    return pl.pallas_call(
        functools.partial(down_kernel, counts=counts, rows=rows // 2),
        out_shape=(out, out),
        grid_spec=pltpu.PrefetchScalarGridSpec(
            num_scalar_prefetch=1,
            grid=(width // tile,),
            in_specs=[pl.BlockSpec(array.shape, lambda n, flags: (0, 0, 0, 0)) for array in flat]
            + [pl.BlockSpec(memory_space=pltpu.VMEM)],
            out_specs=[pl.BlockSpec((rows // 2, tile), lambda n, flags: (0, n))] * 2,
            scratch_shapes=[pltpu.VMEM((rows, experts * hidden), jnp.bfloat16)],
        ),
        cost_estimate=pl.CostEstimate(
            flops=2 * rows * hidden * width * experts,
            bytes_accessed=2 * hidden * width * experts,
            transcendentals=0,
        ),
        compiler_params=pltpu.CompilerParams(vmem_limit_bytes=VMEM),
        name="down",
    )(flags, *flat, w_down)


def merge_kernel(flags, keep_ref, got_ref, out_ref, kept_ref):
    quarter = out_ref.shape[3]

    def part(chip):
        span = pl.ds(pl.multiple_of(chip * quarter, quarter), quarter)
        here = keep_ref[:, :, :, span].astype(jnp.float32)
        return here + got_ref[:, :, :, span].astype(jnp.float32)

    out_ref[...] = part(1 - flags[1]).astype(out_ref.dtype)
    kept_ref[...] = part(flags[1])


def core_sum(keep, got, flags):
    kinds, count, rows, half = keep.shape
    shape = (kinds, count, rows, half // 2)
    spec = pl.BlockSpec((kinds, 1, rows, half), lambda e, flags: (0, e, 0, 0))
    out_spec = pl.BlockSpec((kinds, 1, rows, half // 2), lambda e, flags: (0, e, 0, 0))
    return pl.pallas_call(
        merge_kernel,
        out_shape=(
            jax.ShapeDtypeStruct(shape, jnp.bfloat16),
            jax.ShapeDtypeStruct(shape, jnp.float32),
        ),
        grid_spec=pltpu.PrefetchScalarGridSpec(
            num_scalar_prefetch=1, grid=(count,), in_specs=[spec] * 2, out_specs=(out_spec,) * 2
        ),
        cost_estimate=pl.CostEstimate(
            flops=keep.size, bytes_accessed=7 * keep.size, transcendentals=0
        ),
        compiler_params=pltpu.CompilerParams(vmem_limit_bytes=VMEM),
        name="merge",
    )(flags, keep, got)


def activate_kernel(flags, kept_ref, got_ref, *refs, first, local, active):
    gate_refs, act_ref = refs[:-1], refs[-1]
    rows = gate_refs[0].shape[0]
    which = flags[3] * local + first + pl.program_id(0)
    lane = lax.broadcasted_iota(jnp.int32, gate_refs[0].shape, 1)
    mine = (lane == which) | (lane == which + active)

    def weight(index):
        block = gate_refs[index][...]
        if len(gate_refs) > 2:
            block = jnp.where(flags[2] == 1, block, gate_refs[index + 2][...])
        return jnp.sum(jnp.where(mine, block.astype(jnp.float32), 0.0), axis=1, keepdims=True)

    for index in range(2):
        span = slice(index * rows, (index + 1) * rows)
        gate = kept_ref[0, 0, span] + got_ref[0, 0, span].astype(jnp.float32)
        up = kept_ref[1, 0, span] + got_ref[1, 0, span].astype(jnp.float32)
        act_ref[0, span] = (jax.nn.silu(gate) * up * weight(index)).astype(act_ref.dtype)


def activate(kept, got, parts, flags, first, local, depth):
    kinds, count, rows, quarter = kept.shape
    spec = pl.BlockSpec((kinds, 1, rows, quarter), lambda e, flags: (0, e, 0, 0))
    gate_spec = pl.BlockSpec((rows // 2, LANES), lambda e, flags: (0, depth // LANES))
    return pl.pallas_call(
        functools.partial(activate_kernel, first=first, local=local, active=local * LINE),
        out_shape=jax.ShapeDtypeStruct((count, rows, quarter), jnp.bfloat16),
        grid_spec=pltpu.PrefetchScalarGridSpec(
            num_scalar_prefetch=1,
            grid=(count,),
            in_specs=[spec] * 2 + [gate_spec] * len(parts),
            out_specs=pl.BlockSpec((1, rows, quarter), lambda e, flags: (e, 0, 0)),
        ),
        cost_estimate=pl.CostEstimate(
            flops=4 * kept.size, bytes_accessed=7 * kept.size, transcendentals=kept.size
        ),
        compiler_params=pltpu.CompilerParams(vmem_limit_bytes=VMEM),
        name="activate",
    )(flags, kept, got, *parts)


def spread(act, chip):
    here = jnp.stack([act, chip])
    return here, flip(here, TENSOR, 4, 1)


def layer(
    q_absorbed,
    kv_latent,
    w_values,
    w_out,
    layer_input,
    norm_gain,
    actual,
    gates,
    w_gate,
    w_up,
    w_down,
):
    token_count = layer_input.shape[0]
    local, slice_width, _ = w_gate.shape
    me, side = lax.axis_index(EXPERT), lax.axis_index(TENSOR)
    inner = (me == 1) | (me == 2)
    flags = jnp.stack([side & 1, side >> 1, inner.astype(jnp.int32), me.astype(jnp.int32)])
    inner, first_core, first_chip, flags = lax.optimization_barrier(
        (inner, (side & 1) == 0, (side & 2) == 0, flags)
    )
    own = expert_rows(layer_input, norm_gain, actual, gates, slice_width, local * LINE)
    pair = lax.ppermute(own, EXPERT, OUTER)
    across = lax.ppermute(own, EXPERT, INNER)
    whole, halves = key_halves(after(kv_latent, own), first_core)
    step = local // 2
    early = stage(after((w_gate, w_up), own, flags), 0, step)
    pair, across, early = after((pair, across, early), early)
    beyond = lax.ppermute(pair, EXPERT, INNER)
    out_first = lax.ppermute(across, EXPERT, OUTWARD)


    def turn(parts, weights):
        send = gate_up(parts, flags, *weights, 0)
        got = flip(send, TENSOR, LINE, 1)
        parts = after(parts, send)
        keep = gate_up(parts, flags, *weights, 1)
        out, kept = core_sum(keep, got, flags)
        return out, kept, flip(out, TENSOR, LINE, 2)

    def act(kept, got, parts, first):
        return activate(kept, got, parts, flags, first, local, slice_width)

    def spread_chip(acts):
        return flip(acts, TENSOR, 4, 2)

    out0, kept0, got0 = turn([own, pair], early)
    out_second = lax.ppermute(beyond, EXPERT, OUTWARD)
    late = stage(after((w_gate, w_up), out0), step, step)
    near_own, near_pair = after((own, pair), out0, beyond)
    out1, kept1, got1 = turn([near_own, near_pair], late)
    near = [near_own, near_pair]
    blocks = key_blocks(whole, after(halves, out1), first_core)
    heads_out = attention(q_absorbed, blocks, w_values, flags)
    across, beyond, out_first, out_second = after(
        (across, beyond, out_first, out_second), heads_out
    )
    far = [across, beyond, out_first, out_second]
    pair_heads = lax.ppermute(heads_out, EXPERT, OUTER)
    across_heads = lax.ppermute(heads_out, EXPERT, INNER)
    out2, kept2, got2 = turn(far, early)
    pair_heads, across_heads, far = after((pair_heads, across_heads, far), out2)
    beyond_heads = lax.ppermute(pair_heads, EXPERT, INNER)
    first_heads = lax.ppermute(across_heads, EXPERT, OUTWARD)
    out3, kept3, got3 = turn(far, late)
    beyond_heads, got2, far = after((beyond_heads, got2, far), out3)
    second_heads = lax.ppermute(beyond_heads, EXPERT, OUTWARD)
    act2 = act(kept2, got2, far, 0)
    chip2 = spread_chip(act2)
    got0, got1 = after((got0, got1), act2)
    act0 = act(kept0, got0, near, 0)
    act1 = act(kept1, got1, near, step)
    (down_near,) = stage([after(w_down, act0, act1)], 0, local)
    got3 = after(got3, down_near)
    act3 = act(kept3, got3, far, step)
    chip3 = spread_chip(act3)
    act0, act1 = after((act0, act1), act3)
    chip0 = spread_chip(act0)
    chip1 = spread_chip(act1)
    first_heads, second_heads, beyond_heads = after(
        (first_heads, second_heads, beyond_heads), act3
    )
    slots = jnp.concatenate(
        [
            heads_out,
            pair_heads,
            jnp.where(inner, across_heads, first_heads),
            jnp.where(inner, beyond_heads, second_heads),
        ],
        axis=0,
    )
    partial = jnp.dot(slots, w_out, preferred_element_type=jnp.float32).astype(jnp.bfloat16)
    chip2, chip3 = after((chip2, chip3), partial)
    far_pieces = [spread(act2, chip2), spread(act3, chip3)]
    far_first, far_second = down(far_pieces, flags, down_near)
    in_second = lax.ppermute(far_second, EXPERT, INWARD)
    chip0, chip1 = after((chip0, chip1), far_first)
    near_pieces = [spread(act0, chip0), spread(act1, chip1)]
    near_own, near_pair = down(near_pieces, flags, down_near)
    far_first = after(far_first, near_own)
    in_first = lax.ppermute(far_first, EXPERT, INWARD)
    got_second = lax.ppermute(add(far_second, in_second), EXPERT, INNER)
    got_first = lax.ppermute(add(far_first, in_first), EXPERT, INNER)
    got_pair = lax.ppermute(add(near_pair, got_second), EXPERT, OUTER)
    mixture = (
        near_own.astype(jnp.float32) + got_first.astype(jnp.float32) + got_pair.astype(jnp.float32)
    ).astype(jnp.bfloat16)
    half = 2 * token_count
    mine = partial
    for bit, first in ((1, first_core), (2, first_chip)):
        low, high = mine[:half], mine[half:]
        got = flip(jnp.where(first, high, low), TENSOR, LINE, bit)
        mine = add(jnp.where(first, low, high), got)
        half //= 2
    pairs = []
    for e in range(LINE):
        for t in range(LINE):
            slot = 2 * (t & 1) + (t >> 1)
            pairs.append((e * LINE + t, block_at(e, slot) * LINE + e))
    attended = lax.ppermute(mine, (EXPERT, TENSOR), pairs)
    return attended, mixture


def solution(mesh):
    experts, tensors = mesh.shape[EXPERT], mesh.shape[TENSOR]

    def body(
        q_absorbed,
        kv_latent,
        w_values,
        w_out,
        layer_input,
        norm_gain,
        predicted,
        actual,
        gates,
        w_gate,
        w_up,
        w_down,
    ):
        matched = jnp.any(predicted[:, None, :] == actual[:, :, None], axis=2)
        missed = jnp.sum(jnp.where(matched, 0.0, gates), axis=1)
        if experts == LINE and tensors == LINE:
            attended, mixture = layer(
                q_absorbed,
                kv_latent,
                w_values,
                w_out,
                layer_input,
                norm_gain,
                actual,
                gates,
                w_gate,
                w_up,
                w_down,
            )
            return (attended, mixture, missed)
        mixture = mix(
            layer_input, norm_gain, actual, gates, w_gate, w_up, w_down, experts, tensors
        )
        blocks = [kv_latent]
        for _ in range(1, experts):
            blocks.append(line_send(blocks[-1], EXPERT, experts, 1))
        heads_out = attend(q_absorbed, blocks, w_values)
        attended = project(heads_out, w_out, experts, tensors)
        return (attended, mixture, missed)

    placed = (
        P((GROUP, EXPERT), TENSOR),
        P((GROUP, EXPERT), None),
        P(TENSOR, None, None),
        P(TENSOR, EXPERT),
        P((GROUP, EXPERT), None),
        P(),
        P((GROUP, EXPERT), None),
        P((GROUP, EXPERT), None),
        P((GROUP, EXPERT), None),
        P(EXPERT, TENSOR, None),
        P(EXPERT, TENSOR, None),
        P(EXPERT, None, TENSOR),
    )
    return jax.shard_map(
        body,
        mesh=mesh,
        in_specs=placed,
        out_specs=(
            P((GROUP, EXPERT), TENSOR),
            P((GROUP, EXPERT), TENSOR),
            P((GROUP, EXPERT)),
        ),
        check_vma=False,
    )
```

```python
import functools

import jax
import jax.numpy as jnp
from jax import lax
from jax.experimental import pallas as pl
from jax.experimental.pallas import tpu as pltpu
from jax.sharding import PartitionSpec as P


GROUP, EXPERT, TENSOR = "group", "expert", "tensor"
ROPE = 64
VDIM = 128
LANES = 128

EPS = 1e-06
FLOOR = -1e30


def line_send(value, axis, size, step):
    pairs = [(i, i + step) for i in range(size) if 0 <= i + step < size]
    return lax.ppermute(value, axis, pairs)


def line_gather(value, axis, size):
    me = lax.axis_index(axis)
    rights, lefts = [value], [value]
    for _ in range(1, size):
        rights.append(line_send(rights[-1], axis, size, 1))
        lefts.append(line_send(lefts[-1], axis, size, -1))
    return [value] + [jnp.where(me >= s, rights[s], lefts[size - s]) for s in range(1, size)]


def add(first, second):
    return (first.astype(jnp.float32) + second.astype(jnp.float32)).astype(first.dtype)


def line_scatter(blocks, axis, size):
    right, left = None, None
    for far in range(size - 1, 0, -1):
        out_right, out_left = blocks[size - far], blocks[far]
        if right is not None:
            out_right, out_left = add(out_right, right), add(out_left, left)
        right = line_send(out_right, axis, size, 1)
        left = line_send(out_left, axis, size, -1)
    return (
        blocks[0].astype(jnp.float32) + right.astype(jnp.float32) + left.astype(jnp.float32)
    ).astype(blocks[0].dtype)


def flip(value, axis, size, bit):
    return lax.ppermute(value, axis, [(i, i ^ bit) for i in range(size)])


def halve(value, axis, size, dim):
    me = lax.axis_index(axis)
    bit = 1
    while bit < size:
        half = value.shape[dim] // 2
        low = lax.slice_in_dim(value, 0, half, axis=dim)
        high = lax.slice_in_dim(value, half, 2 * half, axis=dim)
        mine = (me & bit) == 0
        got = flip(jnp.where(mine, high, low), axis, size, bit)
        value = jnp.where(mine, low, high).astype(jnp.float32) + got.astype(jnp.float32)
        bit *= 2
        if bit < size:
            value = value.astype(got.dtype)
    return value


def unhalve(value, axis, size, dim):
    me = lax.axis_index(axis)
    bit = size // 2
    while bit >= 1:
        got = flip(value, axis, size, bit)
        mine = (me & bit) == 0
        value = jnp.concatenate(
            [jnp.where(mine, value, got), jnp.where(mine, got, value)], axis=dim
        )
        bit //= 2
    return value


def attend(q_absorbed, blocks, w_values):
    token_count = q_absorbed.shape[0]
    heads_here, latent_width, _ = w_values.shape
    key_width = blocks[0].shape[1]
    scale = (VDIM + ROPE) ** (-0.5)
    me = lax.axis_index(EXPERT)
    keys = jnp.concatenate(blocks, axis=0)
    queries = q_absorbed.reshape(token_count * heads_here, key_width)
    query_pos = jnp.repeat(jnp.arange(token_count, dtype=jnp.int32), heads_here)
    index = jnp.arange(keys.shape[0], dtype=jnp.int32)
    back, place = index // token_count, index % token_count
    own = (back[None, :] == 0) & (query_pos[:, None] >= place[None, :])
    visible = own | ((back >= 1) & (back <= me))[None, :]
    scores = (
        lax.dot_general(
            queries, keys, (((1,), (1,)), ((), ())), preferred_element_type=jnp.float32
        )
        * scale
    )
    masked = jnp.where(visible, scores, FLOOR)
    largest = jnp.max(masked, axis=1)
    expo = jnp.where(visible, jnp.exp(masked - largest[:, None]), 0.0)
    denominator = jnp.sum(expo, axis=1)
    accum = jnp.dot(
        expo.astype(jnp.bfloat16), keys[:, :latent_width], preferred_element_type=jnp.float32
    )
    latent = (
        (accum / denominator[:, None])
        .astype(jnp.bfloat16)
        .reshape(token_count, heads_here, latent_width)
    )
    heads_out = jnp.einsum(
        "thc,hcv->thv", latent, w_values, preferred_element_type=jnp.float32
    ).astype(jnp.bfloat16)
    return heads_out.reshape(token_count, heads_here * w_values.shape[2])


def project(heads_out, w_out, experts, tensors):
    token_count = heads_out.shape[0]
    slots = jnp.concatenate(line_gather(heads_out, EXPERT, experts), axis=0)
    partial = jnp.dot(slots, w_out, preferred_element_type=jnp.float32).astype(jnp.bfloat16)
    if experts == tensors:
        mine = halve(partial, TENSOR, tensors, 0).astype(jnp.bfloat16)
        bits = tensors.bit_length() - 1
        pairs = []
        for e in range(experts):
            for t in range(tensors):
                slot = int(format(t, "0%db" % bits)[::-1], 2)
                pairs.append((e * tensors + t, (e - slot) % experts * tensors + e))
        return lax.ppermute(mine, (EXPERT, TENSOR), pairs)
    me = lax.axis_index(EXPERT)
    order = (me - jnp.arange(experts)) % experts
    blocks = partial.reshape(experts, token_count, -1)[order].reshape(partial.shape)
    rows = lax.all_to_all(blocks, EXPERT, split_axis=0, concat_axis=1, tiled=True)
    return lax.psum_scatter(rows, TENSOR, scatter_dimension=1, tiled=True)


def expert_rows(layer_input, norm_gain, actual, gates, slice_width, active):
    token_count = layer_input.shape[0]
    first_col = lax.axis_index(TENSOR) * slice_width
    features = layer_input.astype(jnp.float32)
    inverse = lax.rsqrt(jnp.mean(features * features, axis=1, keepdims=True) + EPS)
    mine = lax.dynamic_slice_in_dim(layer_input, first_col, slice_width, 1).astype(jnp.float32)
    gain_mine = lax.dynamic_slice_in_dim(norm_gain, first_col, slice_width, 0)
    normed = (mine * inverse * gain_mine).astype(jnp.bfloat16)
    ids = jnp.arange(active, dtype=jnp.int32)
    dense = jnp.sum(
        jnp.where(actual[:, :, None] == ids[None, None, :], gates[:, :, None], 0.0), axis=1
    )
    high = dense.astype(jnp.bfloat16)
    low = (dense - high.astype(jnp.float32)).astype(jnp.bfloat16)
    width = -(-2 * active // LANES) * LANES
    filler = jnp.zeros((token_count, width - 2 * active), jnp.bfloat16)
    return jnp.concatenate([normed, high, low, filler], axis=1)


def mix(layer_input, norm_gain, actual, gates, w_gate, w_up, w_down, experts, tensors):
    token_count = layer_input.shape[0]
    local, slice_width, hidden = w_gate.shape
    active = local * experts
    me = lax.axis_index(EXPERT)
    rows = expert_rows(layer_input, norm_gain, actual, gates, slice_width, active)
    slots = jnp.concatenate(line_gather(rows, EXPERT, experts), axis=0)
    tokens = slots[:, :slice_width]
    both = slots[:, slice_width : slice_width + 2 * active].astype(jnp.float32)
    weight = both[:, :active] + both[:, active:]
    weight = lax.dynamic_slice_in_dim(weight, me * local, local, 1)
    acts = []
    for e in range(local):
        gate_part = jnp.dot(tokens, w_gate[e], preferred_element_type=jnp.float32)
        up_part = jnp.dot(tokens, w_up[e], preferred_element_type=jnp.float32)
        pair = jnp.stack([gate_part.astype(jnp.bfloat16), up_part.astype(jnp.bfloat16)])
        share = halve(pair, TENSOR, tensors, 2)
        act = jax.nn.silu(share[0]) * share[1] * weight[:, e : e + 1]
        acts.append(unhalve(act.astype(jnp.bfloat16), TENSOR, tensors, 1))
    acts = jnp.concatenate(acts, axis=1)
    partial = jnp.dot(
        acts, w_down.reshape(local * hidden, -1), preferred_element_type=jnp.float32
    ).astype(jnp.bfloat16)
    blocks = partial.reshape(experts, token_count, -1)
    return line_scatter([blocks[s] for s in range(experts)], EXPERT, experts)


def after(value, *others):
    return lax.optimization_barrier((value, others))[0]


LINE = 4
VMEM = 10 * 1024 * 1024
STAGE_VMEM = 30 * 1024 * 1024
OUTER = [(0, 1), (1, 0), (2, 3), (3, 2)]
INNER = [(1, 2), (2, 1)]
OUTWARD = [(1, 0), (2, 3)]
INWARD = [(0, 1), (3, 2)]


def block_at(device, slot):
    far = 2 if device < 2 else 0
    inner, outer = (2, 3) if far == 2 else (1, 0)
    return (device, device ^ 1, inner, outer)[slot]


def attention_kernel(flags, q_ref, even_ref, odd_ref, values_ref, out_ref, shut, *, scale):
    rows, keys = shut.shape
    heads = values_ref.shape[0]
    latent_width = values_ref.shape[1]
    value_width = values_ref.shape[2]
    width = q_ref.shape[1] // heads
    reach = even_ref.shape[1]

    @pl.when(pl.program_id(0) == 0)
    def _():
        query = lax.broadcasted_iota(jnp.int32, (rows, keys), 0)
        key = lax.broadcasted_iota(jnp.int32, (rows, keys), 1)
        open_to = jnp.where(key < rows, query, -1)
        for slot in range(1, keys // rows):
            other = flags[3] ^ slot
            limit = jnp.where(other < flags[3], keys, -1)
            open_to = jnp.where((key >= slot * rows) & (key < (slot + 1) * rows), limit, open_to)
        shut[...] = jnp.where(key <= open_to, 0.0, FLOOR)

    even = [q_ref[:, h * width : h * width + reach] for h in range(0, heads, 2)]
    odd = [q_ref[:, (h + 1) * width - reach : (h + 1) * width] for h in range(1, heads, 2)]
    for parity, group, key_ref in ((0, even, even_ref), (1, odd, odd_ref)):
        queries = jnp.concatenate(group, axis=0)
        scores = lax.dot_general(
            queries, key_ref[...], (((1,), (1,)), ((), ())), preferred_element_type=jnp.float32
        )
        scores = (scores * scale).reshape(len(group), rows, keys) + shut[...][None]
        largest = jnp.max(scores, axis=2, keepdims=True)
        expo = jnp.exp(scores - largest)
        bottom = jnp.sum(expo, axis=2, keepdims=True)
        total = jnp.dot(
            expo.astype(jnp.bfloat16).reshape(len(group) * rows, keys),
            even_ref[:, :latent_width],
            preferred_element_type=jnp.float32,
        ).reshape(len(group), rows, latent_width)
        latent = (total / bottom).astype(jnp.bfloat16)
        for index in range(len(group)):
            head = 2 * index + parity
            out_ref[:, head * value_width : (head + 1) * value_width] = jnp.dot(
                latent[index], values_ref[head], preferred_element_type=jnp.float32
            ).astype(out_ref.dtype)


HEADS_AT_ONCE = 4


def attention(q_absorbed, blocks, w_values, flags):
    rows = q_absorbed.shape[0]
    heads, latent_width, value_width = w_values.shape
    width = q_absorbed.shape[1] // heads
    keys = jnp.concatenate(blocks, axis=0)
    count, reach = keys.shape
    odd = jnp.concatenate(
        [jnp.zeros((count, reach - width), keys.dtype), keys[:, :width]], axis=1
    )
    group = HEADS_AT_ONCE
    flops = 2 * rows * count * (width + latent_width) * heads
    flops += 2 * rows * latent_width * value_width * heads
    return pl.pallas_call(
        functools.partial(attention_kernel, scale=(VDIM + ROPE) ** (-0.5)),
        out_shape=jax.ShapeDtypeStruct((rows, heads * value_width), jnp.bfloat16),
        grid_spec=pltpu.PrefetchScalarGridSpec(
            num_scalar_prefetch=1,
            grid=(heads // group,),
            in_specs=[
                pl.BlockSpec((rows, group * width), lambda h, flags: (0, h)),
                pl.BlockSpec((count, reach), lambda h, flags: (0, 0)),
                pl.BlockSpec((count, reach), lambda h, flags: (0, 0)),
                pl.BlockSpec((group, latent_width, value_width), lambda h, flags: (h, 0, 0)),
            ],
            out_specs=pl.BlockSpec((rows, group * value_width), lambda h, flags: (0, h)),
            scratch_shapes=[pltpu.VMEM((rows, count), jnp.float32)],
        ),
        cost_estimate=pl.CostEstimate(
            flops=flops,
            bytes_accessed=2 * rows * heads * width,
            transcendentals=rows * heads * count,
        ),
        compiler_params=pltpu.CompilerParams(vmem_limit_bytes=VMEM),
        name="attention",
    )(flags, q_absorbed, keys, odd, w_values)


def key_halves(kv_latent, first_core):
    rows, width = kv_latent.shape
    half = rows // 2
    whole = jnp.pad(kv_latent, ((0, 0), (0, -width % LANES)))
    mine = jnp.where(first_core, whole[:half], whole[half:])
    pair = flip(mine, EXPERT, LINE, 1)
    others = flip(jnp.stack([mine, pair]), EXPERT, LINE, 2)
    return whole, jnp.concatenate([pair[None], others])


def key_blocks(whole, got, first_core):
    other = flip(got, TENSOR, LINE, 1)
    full = jnp.concatenate(
        [jnp.where(first_core, got, other), jnp.where(first_core, other, got)], axis=1
    )
    return [whole] + [full[index] for index in range(LINE - 1)]


def rows_kernel(flags, *refs, parts, rows, side):
    part_refs, (gate_ref, up_ref, out_ref, tokens) = refs[:parts], refs[parts:]
    item = pl.program_id(0)

    @pl.when(item == 0)
    def _():
        if parts == 2:
            tokens[:rows] = part_refs[0][...]
            tokens[rows:] = part_refs[1][...]
        else:

            @pl.when(flags[2] == 1)
            def _():
                tokens[:rows] = part_refs[0][...]
                tokens[rows:] = part_refs[1][...]

            @pl.when(flags[2] == 0)
            def _():
                tokens[:rows] = part_refs[2][...]
                tokens[rows:] = part_refs[3][...]

    half = gate_ref.shape[2] // 2
    core = flags[0] if side else 1 - flags[0]
    span = pl.ds(pl.multiple_of(core * half, half), half)
    for index, weight_ref in enumerate((gate_ref, up_ref)):
        out_ref[index, 0] = jnp.dot(
            tokens[...], weight_ref[item, :, span], preferred_element_type=jnp.float32
        ).astype(out_ref.dtype)


def stage_kernel(*refs, first, count):
    half = len(refs) // 2
    sources, targets, sems = refs[:half], refs[half : 2 * half], refs[-1]
    copies = [
        pltpu.make_async_copy(
            sources[which].at[first + item], targets[which].at[item], sems.at[which, item]
        )
        for item in range(count)
        for which in range(half)
    ]
    for copy in copies:
        copy.start()
    for copy in copies:
        copy.wait()


def stage(weights, first, count):
    shapes = [(count,) + weight.shape[1:] for weight in weights]
    size = sum(weight[0].size * count for weight in weights)
    return pl.pallas_call(
        functools.partial(stage_kernel, first=first, count=count),
        out_shape=tuple(pltpu.VMEM(shape, weights[0].dtype) for shape in shapes),
        in_specs=[pl.BlockSpec(memory_space=pltpu.HBM)] * len(weights),
        out_specs=(pl.BlockSpec(memory_space=pltpu.VMEM),) * len(weights),
        scratch_shapes=[pltpu.SemaphoreType.DMA((len(weights), count))],
        cost_estimate=pl.CostEstimate(flops=0, bytes_accessed=2 * size, transcendentals=0),
        compiler_params=pltpu.CompilerParams(vmem_limit_bytes=STAGE_VMEM),
        name="stage",
    )(*weights)


def gate_up(parts, flags, w_gate, w_up, side):
    rows = parts[0].shape[0]
    count, depth, hidden = w_gate.shape
    half = hidden // 2
    return pl.pallas_call(
        functools.partial(rows_kernel, parts=len(parts), rows=rows, side=side),
        out_shape=jax.ShapeDtypeStruct((2, count, 2 * rows, half), jnp.bfloat16),
        grid_spec=pltpu.PrefetchScalarGridSpec(
            num_scalar_prefetch=1,
            grid=(count,),
            in_specs=[pl.BlockSpec((rows, depth), lambda e, flags: (0, 0))] * len(parts)
            + [pl.BlockSpec(memory_space=pltpu.VMEM)] * 2,
            out_specs=pl.BlockSpec((2, 1, 2 * rows, half), lambda e, flags: (0, e, 0, 0)),
            scratch_shapes=[pltpu.VMEM((2 * rows, depth), jnp.bfloat16)],
        ),
        cost_estimate=pl.CostEstimate(
            flops=4 * rows * depth * hidden * count,
            bytes_accessed=2 * depth * hidden * count,
            transcendentals=0,
        ),
        compiler_params=pltpu.CompilerParams(vmem_limit_bytes=VMEM),
        name="gate_up",
    )(flags, *parts, w_gate, w_up)


def down_kernel(flags, *refs, counts, rows):
    pieces, (weight_ref, low_ref, high_ref, acts) = refs[: 2 * len(counts)], refs[2 * len(counts) :]
    quarter = pieces[0].shape[3]

    @pl.when(pl.program_id(0) == 0)
    def _():
        first = 0
        for index, count in enumerate(counts):
            for item in range(count):
                for core in range(2):
                    for chip in range(2):
                        column = (first + item) * 4 + 2 * core + chip
                        span = slice(column * quarter, (column + 1) * quarter)
                        here, there = pieces[2 * index], pieces[2 * index + 1]
                        slot = flags[1] if chip == 0 else 1 - flags[1]

                        @pl.when(flags[0] == core)
                        def _(here=here, span=span, slot=slot, item=item):
                            acts[:, span] = here[slot, item]

                        @pl.when(flags[0] != core)
                        def _(there=there, span=span, slot=slot, item=item):
                            acts[:, span] = there[slot, item]

            first += count

    depth = weight_ref.shape[0] * weight_ref.shape[1]
    tile = low_ref.shape[1]
    span = pl.ds(pl.multiple_of(pl.program_id(0) * tile, tile), tile)
    total = jnp.dot(
        acts[...],
        weight_ref[:, :, span].reshape(depth, tile),
        preferred_element_type=jnp.float32,
    )
    low_ref[...] = total[:rows].astype(low_ref.dtype)
    high_ref[...] = total[rows:].astype(high_ref.dtype)


def down(pieces, flags, w_down):
    counts = [here.shape[1] for here, _ in pieces]
    _, _, rows, _ = pieces[0][0].shape
    experts, hidden, width = w_down.shape
    tile = 2 * LANES if width % (2 * LANES) == 0 else LANES
    flat = [array for pair in pieces for array in pair]
    out = jax.ShapeDtypeStruct((rows // 2, width), jnp.bfloat16)
    return pl.pallas_call(
        functools.partial(down_kernel, counts=counts, rows=rows // 2),
        out_shape=(out, out),
        grid_spec=pltpu.PrefetchScalarGridSpec(
            num_scalar_prefetch=1,
            grid=(width // tile,),
            in_specs=[pl.BlockSpec(array.shape, lambda n, flags: (0, 0, 0, 0)) for array in flat]
            + [pl.BlockSpec(memory_space=pltpu.VMEM)],
            out_specs=[pl.BlockSpec((rows // 2, tile), lambda n, flags: (0, n))] * 2,
            scratch_shapes=[pltpu.VMEM((rows, experts * hidden), jnp.bfloat16)],
        ),
        cost_estimate=pl.CostEstimate(
            flops=2 * rows * hidden * width * experts,
            bytes_accessed=2 * hidden * width * experts,
            transcendentals=0,
        ),
        compiler_params=pltpu.CompilerParams(vmem_limit_bytes=VMEM),
        name="down",
    )(flags, *flat, w_down)


def merge_kernel(flags, keep_ref, got_ref, out_ref, kept_ref):
    quarter = out_ref.shape[3]

    def part(chip):
        span = pl.ds(pl.multiple_of(chip * quarter, quarter), quarter)
        here = keep_ref[:, :, :, span].astype(jnp.float32)
        return here + got_ref[:, :, :, span].astype(jnp.float32)

    out_ref[...] = part(1 - flags[1]).astype(out_ref.dtype)
    kept_ref[...] = part(flags[1])


def core_sum(keep, got, flags):
    kinds, count, rows, half = keep.shape
    shape = (kinds, count, rows, half // 2)
    spec = pl.BlockSpec((kinds, 1, rows, half), lambda e, flags: (0, e, 0, 0))
    out_spec = pl.BlockSpec((kinds, 1, rows, half // 2), lambda e, flags: (0, e, 0, 0))
    return pl.pallas_call(
        merge_kernel,
        out_shape=(
            jax.ShapeDtypeStruct(shape, jnp.bfloat16),
            jax.ShapeDtypeStruct(shape, jnp.float32),
        ),
        grid_spec=pltpu.PrefetchScalarGridSpec(
            num_scalar_prefetch=1, grid=(count,), in_specs=[spec] * 2, out_specs=(out_spec,) * 2
        ),
        cost_estimate=pl.CostEstimate(
            flops=keep.size, bytes_accessed=7 * keep.size, transcendentals=0
        ),
        compiler_params=pltpu.CompilerParams(vmem_limit_bytes=VMEM),
        name="merge",
    )(flags, keep, got)


def activate_kernel(flags, kept_ref, got_ref, *refs, first, local, active):
    gate_refs, act_ref = refs[:-1], refs[-1]
    rows = gate_refs[0].shape[0]
    which = flags[3] * local + first + pl.program_id(0)
    lane = lax.broadcasted_iota(jnp.int32, gate_refs[0].shape, 1)
    mine = (lane == which) | (lane == which + active)

    def weight(index):
        block = gate_refs[index][...]
        if len(gate_refs) > 2:
            block = jnp.where(flags[2] == 1, block, gate_refs[index + 2][...])
        return jnp.sum(jnp.where(mine, block.astype(jnp.float32), 0.0), axis=1, keepdims=True)

    for index in range(2):
        span = slice(index * rows, (index + 1) * rows)
        gate = kept_ref[0, 0, span] + got_ref[0, 0, span].astype(jnp.float32)
        up = kept_ref[1, 0, span] + got_ref[1, 0, span].astype(jnp.float32)
        act_ref[0, span] = (jax.nn.silu(gate) * up * weight(index)).astype(act_ref.dtype)


def activate(kept, got, parts, flags, first, local, depth):
    kinds, count, rows, quarter = kept.shape
    spec = pl.BlockSpec((kinds, 1, rows, quarter), lambda e, flags: (0, e, 0, 0))
    gate_spec = pl.BlockSpec((rows // 2, LANES), lambda e, flags: (0, depth // LANES))
    return pl.pallas_call(
        functools.partial(activate_kernel, first=first, local=local, active=local * LINE),
        out_shape=jax.ShapeDtypeStruct((count, rows, quarter), jnp.bfloat16),
        grid_spec=pltpu.PrefetchScalarGridSpec(
            num_scalar_prefetch=1,
            grid=(count,),
            in_specs=[spec] * 2 + [gate_spec] * len(parts),
            out_specs=pl.BlockSpec((1, rows, quarter), lambda e, flags: (e, 0, 0)),
        ),
        cost_estimate=pl.CostEstimate(
            flops=4 * kept.size, bytes_accessed=7 * kept.size, transcendentals=kept.size
        ),
        compiler_params=pltpu.CompilerParams(vmem_limit_bytes=VMEM),
        name="activate",
    )(flags, kept, got, *parts)


def spread(act, chip):
    here = jnp.stack([act, chip])
    return here, flip(here, TENSOR, 4, 1)


def layer(
    q_absorbed,
    kv_latent,
    w_values,
    w_out,
    layer_input,
    norm_gain,
    actual,
    gates,
    w_gate,
    w_up,
    w_down,
):
    token_count = layer_input.shape[0]
    local, slice_width, _ = w_gate.shape
    me, side = lax.axis_index(EXPERT), lax.axis_index(TENSOR)
    inner = (me == 1) | (me == 2)
    flags = jnp.stack([side & 1, side >> 1, inner.astype(jnp.int32), me.astype(jnp.int32)])
    inner, first_core, first_chip, flags = lax.optimization_barrier(
        (inner, (side & 1) == 0, (side & 2) == 0, flags)
    )
    own = expert_rows(layer_input, norm_gain, actual, gates, slice_width, local * LINE)
    pair = lax.ppermute(own, EXPERT, OUTER)
    across = lax.ppermute(own, EXPERT, INNER)
    whole, halves = key_halves(after(kv_latent, own), first_core)
    step = local // 2
    early = stage(after((w_gate, w_up), own, flags), 0, step)
    pair, early = after((pair, early), early)

    def act(kept, got, parts, first):
        return activate(kept, got, parts, flags, first, local, slice_width)

    def turn(parts, weights, pending=()):
        send = gate_up(parts, flags, *weights, 0)
        got = flip(send, TENSOR, LINE, 1)
        parts, pending = after((parts, pending), send)
        keep = gate_up(parts, flags, *weights, 1)
        out, kept = core_sum(keep, got, flags)
        return (out, kept, flip(out, TENSOR, LINE, 2)), pending

    def spread_chip(acts):
        return flip(acts, TENSOR, LINE, 2)

    (out0, kept0, got0), (pair_on, across) = turn([own, pair], early, (pair, across))
    beyond = lax.ppermute(pair_on, EXPERT, INNER)
    out_first = lax.ppermute(across, EXPERT, OUTWARD)
    late = stage(after((w_gate, w_up), out0), step, step)
    near_own, near_pair, beyond = after((own, pair, beyond), late)
    out_second = lax.ppermute(beyond, EXPERT, OUTWARD)
    (out1, kept1, got1), _ = turn([near_own, near_pair], late)
    near = [near_own, near_pair]
    blocks = key_blocks(whole, after(halves, out1), first_core)
    heads_out = attention(q_absorbed, blocks, w_values, flags)
    across, beyond, out_first, out_second = after(
        (across, beyond, out_first, out_second), heads_out
    )
    far = [across, beyond, out_first, out_second]
    pair_heads = lax.ppermute(heads_out, EXPERT, OUTER)
    across_heads = lax.ppermute(heads_out, EXPERT, INNER)
    (out2, kept2, got2), _ = turn(far, early)
    far = after(far, out2)
    (out3, kept3, got3), _ = turn(far, late)
    pair_heads, across_heads, got2, far = after((pair_heads, across_heads, got2, far), out3)
    beyond_heads = lax.ppermute(pair_heads, EXPERT, INNER)
    first_heads = lax.ppermute(across_heads, EXPERT, OUTWARD)
    act2 = act(kept2, got2, far, 0)
    chip2 = spread_chip(act2)
    got0, got1 = after((got0, got1), act2)
    act0 = act(kept0, got0, near, 0)
    act1 = act(kept1, got1, near, step)
    acts = jnp.concatenate([act0, act1])
    (down_near,) = stage([after(w_down, acts)], 0, local)
    got3, beyond_heads = after((got3, beyond_heads), down_near)
    act3 = act(kept3, got3, far, step)
    chip3 = spread_chip(act3)
    acts = after(acts, act3)
    chip0 = spread_chip(acts)
    second_heads = lax.ppermute(beyond_heads, EXPERT, OUTWARD)
    far_pieces = [spread(act2, chip2), spread(act3, chip3)]
    far_first, far_second = down(far_pieces, flags, down_near)
    in_second = lax.ppermute(far_second, EXPERT, INWARD)
    first_heads, second_heads, beyond_heads = after(
        (first_heads, second_heads, beyond_heads), far_second
    )
    slots = jnp.concatenate(
        [
            heads_out,
            pair_heads,
            jnp.where(inner, across_heads, first_heads),
            jnp.where(inner, beyond_heads, second_heads),
        ],
        axis=0,
    )
    partial = jnp.dot(slots, w_out, preferred_element_type=jnp.float32).astype(jnp.bfloat16)
    acts, chip0 = after((acts, chip0), partial)
    near_pieces = [spread(acts, chip0)]
    near_own, near_pair = down(near_pieces, flags, down_near)
    far_first = after(far_first, near_own)
    in_first = lax.ppermute(far_first, EXPERT, INWARD)
    got_second = lax.ppermute(add(far_second, in_second), EXPERT, INNER)
    got_first = lax.ppermute(add(far_first, in_first), EXPERT, INNER)
    got_pair = lax.ppermute(add(near_pair, got_second), EXPERT, OUTER)
    mixture = (
        near_own.astype(jnp.float32) + got_first.astype(jnp.float32) + got_pair.astype(jnp.float32)
    ).astype(jnp.bfloat16)
    half = 2 * token_count
    mine = partial
    for bit, first in ((1, first_core), (2, first_chip)):
        low, high = mine[:half], mine[half:]
        got = flip(jnp.where(first, high, low), TENSOR, LINE, bit)
        mine = add(jnp.where(first, low, high), got)
        half //= 2
    pairs = []
    for e in range(LINE):
        for t in range(LINE):
            slot = 2 * (t & 1) + (t >> 1)
            pairs.append((e * LINE + t, block_at(e, slot) * LINE + e))
    attended = lax.ppermute(mine, (EXPERT, TENSOR), pairs)
    return attended, mixture


def solution(mesh):
    experts, tensors = mesh.shape[EXPERT], mesh.shape[TENSOR]

    def body(
        q_absorbed,
        kv_latent,
        w_values,
        w_out,
        layer_input,
        norm_gain,
        predicted,
        actual,
        gates,
        w_gate,
        w_up,
        w_down,
    ):
        matched = jnp.any(predicted[:, None, :] == actual[:, :, None], axis=2)
        missed = jnp.sum(jnp.where(matched, 0.0, gates), axis=1)
        if experts == LINE and tensors == LINE:
            attended, mixture = layer(
                q_absorbed,
                kv_latent,
                w_values,
                w_out,
                layer_input,
                norm_gain,
                actual,
                gates,
                w_gate,
                w_up,
                w_down,
            )
            return (attended, mixture, missed)
        mixture = mix(
            layer_input, norm_gain, actual, gates, w_gate, w_up, w_down, experts, tensors
        )
        blocks = [kv_latent]
        for _ in range(1, experts):
            blocks.append(line_send(blocks[-1], EXPERT, experts, 1))
        heads_out = attend(q_absorbed, blocks, w_values)
        attended = project(heads_out, w_out, experts, tensors)
        return (attended, mixture, missed)

    placed = (
        P((GROUP, EXPERT), TENSOR),
        P((GROUP, EXPERT), None),
        P(TENSOR, None, None),
        P(TENSOR, EXPERT),
        P((GROUP, EXPERT), None),
        P(),
        P((GROUP, EXPERT), None),
        P((GROUP, EXPERT), None),
        P((GROUP, EXPERT), None),
        P(EXPERT, TENSOR, None),
        P(EXPERT, TENSOR, None),
        P(EXPERT, None, TENSOR),
    )
    return jax.shard_map(
        body,
        mesh=mesh,
        in_specs=placed,
        out_specs=(
            P((GROUP, EXPERT), TENSOR),
            P((GROUP, EXPERT), TENSOR),
            P((GROUP, EXPERT)),
        ),
        check_vma=False,
    )
```
